128 devices in a mesh: grp: 8 (over y, core), dev: 16 (over x, z).
Axes of the slice: x: 4, y: 4, z: 4, core: 2. Of those that a mesh axis runs over, the one named last changes fastest.
Arguments:
- tiles: bfloat16 [65536, 128, 128], P(('grp', 'dev')), may hold values from -0.125 to 0.125
- tile_ray: int32 [65536], P(('grp', 'dev')), may hold values from 0 to 31, as said below
- tile_col: int32 [65536], P(('grp', 'dev')), may hold values from 0 to 23, as said below
- touched: int32 [3072], P(('grp', 'dev')), may hold values from 0 to 8191, as said below
- home: int32 [8192], replicated, may hold values from 0 to 8191, as said below
- sketch: bfloat16 [1048576, 128], P(('grp', 'dev')), may hold values from -6 to 6
Outputs:
- basis: float32 [1048576, 128], P(('grp', 'dev'))
- r_factor: float32 [128, 128], replicated
The draws below stay inside these ranges and needn't reach their ends.
Inputs may be any that keep to these rules, and one draw needn't show every extreme that they name: `home`: A permutation that maps each region of 1024 consecutive voxel blocks, g * 1024 to (g + 1) * 1024 - 1, onto the same range of positions. The 24 entries of device i along grp+dev are distinct voxel blocks whose positions home[v] lie in the region of its group g = i // 16; at most 3 of them have positions stored on any one device (position // 64), and in every group one device stores 3 of the touched blocks of every device of the group. On each device the pairs (tile_ray, tile_col) are distinct. `tile_col`: indexes the device's own 24 entries of touched.
All inputs are finite; a program needn't handle non-finite values.
Results may differ from the reference program's by a relative error of at most 0.0017.
Values may be sent and summed in bfloat16 or wider, within the bound.
A program may use at most 192 MiB of HBM per device.

```python
import math
import jax
import jax.numpy as jnp
from jax import lax

BLK = 128
K = 128
VBLK_DEV = 64
NTOUCH = 24
CAP = 3
TILES_RB = 16
RB_DEV = 32
NT_DEV = 512
REGION = 1024
VBLOCKS = 8192
VOX = 1048576
RAYBLK = 4096
TILES = 65536
DEVICES = 128


def pair_table(key):
    base = jax.random.fold_in(key, 31)

    def single(index):
        return jax.random.permutation(jax.random.fold_in(base, index), RB_DEV * NTOUCH)[:NT_DEV]
    return jax.vmap(single)(jnp.arange(DEVICES)).reshape(-1).astype(jnp.int32)


def draw_tile_ray(key, part):
    return (pair_table(key) // NTOUCH).astype(jnp.int32)


def draw_tile_col(key, part):
    return (pair_table(key) % NTOUCH).astype(jnp.int32)


def region_layout(key):
    base = jax.random.fold_in(key, 53)
    groups = VBLOCKS // REGION

    def single(group):
        return jax.random.permutation(jax.random.fold_in(base, group), REGION)
    perms = jax.vmap(single)(jnp.arange(groups))
    home_map = (perms + (jnp.arange(groups) * REGION)[:, None]).reshape(-1).astype(jnp.int32)
    inverse = jnp.zeros((VBLOCKS,), jnp.int32).at[home_map].set(jnp.arange(VBLOCKS, dtype=jnp.int32))
    return (home_map, inverse)


def draw_home(key, part):
    return region_layout(key)[0]


def draw_touched(key, part):
    home_map, inverse = region_layout(key)
    base = jax.random.fold_in(key, 71)
    group_size = REGION // VBLK_DEV
    items = group_size * CAP

    def single(device):
        group = device // group_size
        hot = jax.random.randint(jax.random.fold_in(jax.random.fold_in(base, 1), group), (), 0, group_size)
        dev_key = jax.random.fold_in(jax.random.fold_in(base, 2), device)
        order = jax.random.permutation(jax.random.fold_in(dev_key, 0), items)
        score = jnp.zeros((items,), jnp.int32).at[order].set(jnp.arange(items, dtype=jnp.int32))
        item_ids = jnp.arange(items, dtype=jnp.int32)
        score = jnp.where(item_ids // CAP == hot, item_ids % CAP - CAP, score)
        chosen = jnp.argsort(score)[:NTOUCH]
        shuffle = jax.random.permutation(jax.random.fold_in(jax.random.fold_in(dev_key, 3), 0), NTOUCH)
        chosen = chosen[shuffle]
        row_key = jax.random.fold_in(dev_key, 5)
        local_rows = jax.vmap(lambda holder: jax.random.permutation(jax.random.fold_in(row_key, holder), VBLK_DEV)[:CAP])(jnp.arange(group_size))
        holder = chosen // CAP
        local = local_rows[holder, chosen % CAP]
        stored = group * REGION + holder * VBLK_DEV + local
        return inverse[stored]
    return jax.vmap(single)(jnp.arange(DEVICES)).reshape(-1).astype(jnp.int32)


def shard_levels(key, shape, cuts, low, top_value):
    def one(dim, blocks):
        steps = jax.random.uniform(jax.random.fold_in(jax.random.fold_in(key, 6), dim), (blocks,), jnp.float32, low / len(cuts), top_value / len(cuts))
        return jnp.repeat(jnp.exp(steps), shape[dim] // blocks).reshape((-1,) + (1,) * (len(shape) - dim - 1))

    level = one(*cuts[0])
    for cut in cuts[1:]:
        level = level * one(*cut)
    return level


def centred(stream_key, shape, scale, reach, split=(), held_as=jnp.bfloat16):
    array = scale * jax.random.normal(stream_key, shape, jnp.float32)
    if split:
        array = array * shard_levels(stream_key, shape, split, -0.22, 0.18)
    return jnp.clip(array, -reach, reach).astype(held_as)


def setup_inputs(seed: int = 0) -> dict:
    seeds = jax.random.split(jax.random.key(seed), 7)
    return {
        "tiles": centred(seeds[0], (TILES, BLK, BLK), (TILES_RB * BLK) ** -0.5, 0.125, ((0, 128),)),
        "tile_ray": draw_tile_ray(jax.random.fold_in(seeds[6], 71), 0),
        "tile_col": draw_tile_col(jax.random.fold_in(seeds[6], 71), 0),
        "touched": draw_touched(jax.random.fold_in(seeds[6], 71), 0),
        "home": draw_home(jax.random.fold_in(seeds[6], 71), 0),
        "sketch": centred(seeds[5], (VOX, K), 1.0, 6.0, ((0, 128),)),
    }


gram_shift = 0.001

def reference(tiles, tile_ray, tile_col, touched, home, sketch):
    tile_size = tiles.shape[1]
    width = sketch.shape[1]
    device = jnp.arange(TILES, dtype=jnp.int32) // NT_DEV
    ray_global = (device * RB_DEV + tile_ray).astype(jnp.int32)
    voxel_block = touched[(device * NTOUCH + tile_col).astype(jnp.int32)]
    position = home[voxel_block].astype(jnp.int32)
    sketch_blocks = sketch.reshape(VBLOCKS, tile_size, width)
    batch_rows = math.gcd(TILES, 512)
    rounds = TILES // batch_rows
    tile_steps = tiles.reshape(rounds, batch_rows, tile_size, tile_size)
    ray_steps = ray_global.reshape(rounds, batch_rows)
    pos_steps = position.reshape(rounds, batch_rows)

    def image_step(running, inputs):
        tile_block, ray_block, pos_block = inputs
        gathered = sketch_blocks[pos_block].astype(jnp.float32)
        product = jnp.einsum('tab,tbk->tak', tile_block.astype(jnp.float32), gathered, precision=lax.Precision.HIGHEST)
        return (running.at[ray_block].add(product), None)
    images, _ = lax.scan(image_step, jnp.zeros((RAYBLK, tile_size, width), jnp.float32), (tile_steps, ray_steps, pos_steps))
    images = images.astype(jnp.bfloat16)

    def normal_step(running, inputs):
        tile_block, ray_block, pos_block = inputs
        gathered = images[ray_block].astype(jnp.float32)
        product = jnp.einsum('tab,tak->tbk', tile_block.astype(jnp.float32), gathered, precision=lax.Precision.HIGHEST)
        return (running.at[pos_block].add(product), None)
    normal, _ = lax.scan(normal_step, jnp.zeros((VBLOCKS, tile_size, width), jnp.float32), (tile_steps, ray_steps, pos_steps))
    normal = normal.reshape(VOX, width)
    gram_matrix = jnp.dot(normal.T, normal, precision=lax.Precision.HIGHEST) / VOX + gram_shift * jnp.eye(width, dtype=jnp.float32)
    r_factor = jnp.linalg.cholesky(gram_matrix).T
    inverse = jax.scipy.linalg.solve_triangular(r_factor, jnp.eye(width, dtype=jnp.float32), lower=False)
    basis_out = jnp.dot(normal, inverse, precision=lax.Precision.HIGHEST)
    return (basis_out, r_factor)
```

```python
import functools

import jax
import jax.numpy as jnp
from jax import lax
from jax.experimental import pallas as pl
from jax.experimental.pallas import tpu as pltpu
from jax.sharding import PartitionSpec as P

CAP = 3
RB_DEV = 32
BLK = 128
SIDE = 4
GROUP = SIDE * SIDE
SLOTS = GROUP * CAP
gram_shift = 0.001

MESH = pl.DeviceIdType.MESH
SMEM = pltpu.SMEM
VMEM = pltpu.VMEM
f32 = jnp.float32
bf16 = jnp.bfloat16


def vm():
    return pl.BlockSpec(memory_space=VMEM)


def sm():
    return pl.BlockSpec(memory_space=SMEM)


def hbm():
    return pl.BlockSpec(memory_space=pl.ANY)


def prep_kernel(block_count, touched, home, ray, col, req, slot, table, count):
    ntouch = touched.shape[0]
    ntiles = ray.shape[0]

    def init_count(i, c):
        count[i] = 0
        return c

    def init_req(i, c):
        req[i] = -1
        return c

    def init_table(i, c):
        table[i] = ntiles
        return c

    lax.fori_loop(0, GROUP, init_count, 0, unroll=True)
    lax.fori_loop(0, SLOTS, init_req, 0, unroll=True)
    lax.fori_loop(0, RB_DEV * ntouch, init_table, 0, unroll=16)

    def place(j, c):
        stored = home[touched[j]]
        holder = lax.rem(lax.div(stored, block_count), GROUP)
        n = count[holder]
        count[holder] = n + 1
        s = holder * CAP + n
        slot[j] = s
        req[s] = lax.rem(stored, block_count)
        return c

    lax.fori_loop(0, ntouch, place, 0)

    def fill(t, c):
        table[ray[t] * ntouch + col[t]] = t
        return c

    lax.fori_loop(0, ntiles, fill, 0, unroll=16)


OFFSETS = [(dx, dz) for dx in range(SIDE) for dz in range(SIDE) if (dx, dz) != (0, 0)]


def peer_of(me, dx, dz):
    x, z = lax.div(me, SIDE), lax.rem(me, SIDE)
    return lax.rem(x + dx, SIDE) * SIDE + lax.rem(z + dz, SIDE)


def plane_barrier(me):
    barrier = pltpu.get_barrier_semaphore()
    for dx, dz in OFFSETS:
        pl.semaphore_signal(
            barrier, inc=1, device_id={"dev": peer_of(me, dx, dz)}, device_id_type=MESH
        )
    pl.semaphore_wait(barrier, GROUP - 1)


def fetch_kernel(
    req, sketch, got, incoming, ask, asked, asked_s, packed, send, recv, asend, arecv, lsem
):
    me = lax.axis_index("dev")
    lane = lax.broadcasted_iota(jnp.int32, (8, BLK), 1)
    for p in range(GROUP):
        ask[p] = jnp.where(
            lane == 0, req[3 * p], jnp.where(lane == 1, req[3 * p + 1], req[3 * p + 2])
        )
    plane_barrier(me)
    asks = []
    for i, (dx, dz) in enumerate(OFFSETS):
        p = peer_of(me, dx, dz)
        c = pltpu.make_async_remote_copy(
            src_ref=ask.at[p],
            dst_ref=asked.at[me],
            send_sem=asend.at[i],
            recv_sem=arecv.at[i],
            device_id={"dev": p},
            device_id_type=MESH,
        )
        c.start()
        asks.append(c)
    asked[me] = ask[me]
    for c in asks:
        c.wait()
    local = pltpu.make_async_copy(asked, asked_s, lsem)
    local.start()
    local.wait()

    copies = []
    for i, (dx, dz) in enumerate(OFFSETS):
        p = peer_of(me, dx, dz)
        for k in range(CAP):
            packed[p, k] = sketch[jnp.maximum(asked_s[p, 0, k], 0)]
        c = pltpu.make_async_remote_copy(
            src_ref=packed.at[p],
            dst_ref=got.at[me],
            send_sem=send.at[i],
            recv_sem=recv.at[i],
            device_id={"dev": p},
            device_id_type=MESH,
        )
        c.start()
        copies.append(c)
    for k in range(CAP):
        got[me, k] = sketch[jnp.maximum(asked_s[me, 0, k], 0)]
    for p in range(GROUP):
        for k in range(CAP):
            incoming[CAP * p + k] = asked_s[p, 0, k]
    for c in copies:
        c.wait()


def exchange_kernel(out, arrived, send, recv):
    me = lax.axis_index("dev")
    plane_barrier(me)
    copies = []
    for i, (dx, dz) in enumerate(OFFSETS):
        p = peer_of(me, dx, dz)
        c = pltpu.make_async_remote_copy(
            src_ref=out.at[p],
            dst_ref=arrived.at[me],
            send_sem=send.at[i],
            recv_sem=recv.at[i],
            device_id={"dev": p},
            device_id_type=MESH,
        )
        c.start()
        copies.append(c)
    arrived[me] = out[me]
    for c in copies:
        c.wait()


def apply_kernel(ntouch, table, slot, tiles, xs, out, held, xc, images_t, sem):
    ntiles = tiles.shape[0]
    chunks = 8
    step = ntiles // chunks
    loads = []
    for i in range(chunks):
        c = pltpu.make_async_copy(
            tiles.at[pl.ds(i * step, step)], held.at[pl.ds(i * step, step)], sem.at[i]
        )
        c.start()
        loads.append(c)
    held[ntiles] = jnp.zeros((BLK, BLK), bf16)
    for c in range(ntouch):
        xc[pl.ds(c * BLK, BLK), :] = xs[slot[c]]
    for c in loads:
        c.wait()

    per = 2

    def image_step(g, carry):
        rows = [
            jnp.concatenate(
                [held[table[(g * per + i) * ntouch + c]] for c in range(ntouch)], axis=1
            )
            for i in range(per)
        ]
        lhs = jnp.concatenate(rows, axis=0)
        got = jnp.dot(lhs, xc[...], preferred_element_type=f32)
        start = pl.multiple_of(g * (per * BLK), per * BLK)
        images_t[:, pl.ds(start, per * BLK)] = got.T.astype(bf16)
        return carry

    lax.fori_loop(0, RB_DEV // per, image_step, 0)

    def normal_step(g, carry):
        cols = [
            jnp.concatenate(
                [held[table[r * ntouch + g * 2 + i]] for r in range(RB_DEV)], axis=0
            )
            for i in range(2)
        ]
        rhs = jnp.concatenate(cols, axis=1)
        part = jnp.dot(images_t[...], rhs, preferred_element_type=f32)
        for i in range(2):
            out[slot[g * 2 + i]] = part[:, i * BLK : (i + 1) * BLK].T.astype(bf16)
        return carry

    lax.fori_loop(0, ntouch // 2, normal_step, 0)


def split(value):
    high = value.astype(bf16)
    return high, (value - high.astype(f32)).astype(bf16)


def gather_kernel(incoming, arrived, normal, gram):
    normal[...] = jnp.zeros_like(normal)

    def add(s, c):
        row = incoming[s]

        @pl.when(row >= 0)
        def _():
            normal[row] = normal[row] + arrived[s].astype(f32)

        return c

    lax.fori_loop(0, SLOTS, add, 0)

    gram[...] = jnp.zeros_like(gram)
    blocks = normal.shape[0]
    per = 8

    def accumulate(g, c):
        rows = normal[pl.ds(g * per, per)].reshape(per * BLK, BLK)
        high, low = split(rows)
        both = jnp.concatenate([high, low], axis=1)
        part = lax.dot_general(
            high, both, (((0,), (0,)), ((), ())), preferred_element_type=f32
        )
        gram[...] += part
        return c

    lax.fori_loop(0, blocks // per, accumulate, 0)


def reduce_kernel(voxels, both, total, mine, first, part, second, s1, r1, s2, r2, s3, r3):
    me = lax.axis_index("dev")
    grp = lax.axis_index("grp")
    groups = lax.axis_size("grp")
    cross = both[:, BLK:]
    mine[...] = (both[:, :BLK] + cross + cross.T).reshape(mine.shape)

    barrier = pltpu.get_barrier_semaphore()
    for dx, dz in OFFSETS:
        pl.semaphore_signal(
            barrier, inc=1, device_id={"dev": peer_of(me, dx, dz)}, device_id_type=MESH
        )
    for o in range(1, groups):
        pl.semaphore_signal(
            barrier, inc=1, device_id={"grp": lax.rem(grp + o, groups)}, device_id_type=MESH
        )
    pl.semaphore_wait(barrier, GROUP - 1 + groups - 1)

    copies = []
    for i, (dx, dz) in enumerate(OFFSETS):
        p = peer_of(me, dx, dz)
        c = pltpu.make_async_remote_copy(
            src_ref=mine.at[p],
            dst_ref=first.at[me],
            send_sem=s1.at[i],
            recv_sem=r1.at[i],
            device_id={"dev": p},
            device_id_type=MESH,
        )
        c.start()
        copies.append(c)
    first[me] = mine[me]
    for c in copies:
        c.wait()
    chunk = first[0]
    for p in range(1, GROUP):
        chunk = chunk + first[p]
    part[...] = chunk

    copies = []
    for o in range(1, groups):
        g = lax.rem(grp + o, groups)
        c = pltpu.make_async_remote_copy(
            src_ref=part,
            dst_ref=second.at[grp],
            send_sem=s2.at[o - 1],
            recv_sem=r2.at[o - 1],
            device_id={"grp": g},
            device_id_type=MESH,
        )
        c.start()
        copies.append(c)
    second[grp] = chunk
    for c in copies:
        c.wait()
    chunk = second[0]
    for g in range(1, groups):
        chunk = chunk + second[g]
    total[me] = chunk / voxels

    copies = []
    for i, (dx, dz) in enumerate(OFFSETS):
        p = peer_of(me, dx, dz)
        c = pltpu.make_async_remote_copy(
            src_ref=total.at[me],
            dst_ref=total.at[me],
            send_sem=s3.at[i],
            recv_sem=r3.at[i],
            device_id={"dev": p},
            device_id_type=MESH,
        )
        c.start()
        copies.append(c)
    for c in copies:
        c.wait()


def factor(gram):
    n = gram.shape[0]
    bands = n // 8
    row_id = lax.broadcasted_iota(jnp.int32, (8, n), 0)
    lane_id = lax.broadcasted_iota(jnp.int32, (8, n), 1)
    g = [gram[8 * b : 8 * b + 8, :] for b in range(bands)]
    w = [jnp.where(lane_id == row_id + 8 * b, 1.0, 0.0).astype(f32) for b in range(bands)]
    r_bands, w_bands = [], []
    for b in range(bands):
        r_out = jnp.zeros((8, n), f32)
        w_out = jnp.zeros((8, n), f32)
        for k in range(8):
            j = 8 * b + k
            g_row = jnp.broadcast_to(g[b][k : k + 1, :], (8, n))
            w_row = jnp.broadcast_to(w[b][k : k + 1, :], (8, n))
            pivot = jnp.broadcast_to(g_row[:, j : j + 1], (8, n))
            scale = 1.0 / pivot
            g_s = g_row * scale
            w_s = w_row * scale
            for t in range(b, bands):
                factor_t = jnp.broadcast_to(g[t][:, j : j + 1], (8, n))
                if t == b:
                    if k == 7:
                        continue
                    factor_t = jnp.where(row_id > k, factor_t, 0.0)
                g[t] = g[t] - factor_t * g_s
                w[t] = w[t] - factor_t * w_s
            root = jnp.sqrt(pivot)
            r_out = jnp.where(row_id == k, g_s * root, r_out)
            w_out = jnp.where(row_id == k, w_s * root, w_out)
        r_bands.append(jnp.where(lane_id >= row_id + 8 * b, r_out, 0.0))
        w_bands.append(w_out)
    return jnp.concatenate(r_bands, axis=0), jnp.concatenate(w_bands, axis=0)


def basis_kernel(total, normal, basis, r_factor, inverse):
    @pl.when(pl.program_id(0) == 0)
    def _():
        rows = lax.broadcasted_iota(jnp.int32, (BLK, BLK), 0)
        cols = lax.broadcasted_iota(jnp.int32, (BLK, BLK), 1)
        gram = total[...].reshape(BLK, BLK)
        gram = gram + jnp.where(rows == cols, gram_shift, 0.0).astype(f32)
        r_value, lower_inverse = factor(gram)
        r_factor[...] = r_value
        high, low = split(lower_inverse.T)
        inverse[:BLK, :BLK] = high
        inverse[BLK:, :BLK] = high
        inverse[:BLK, BLK:] = low
        inverse[BLK:, BLK:] = jnp.zeros_like(low)

    high, low = split(normal[...])
    got = jnp.dot(
        jnp.concatenate([high, low], axis=1), inverse[...], preferred_element_type=f32
    )
    basis[...] = got[:, :BLK] + got[:, BLK:]


def local(tiles, tile_ray, tile_col, touched, home, sketch):
    block_count = sketch.shape[0] // BLK
    ntouch = touched.shape[0]
    ntiles = tiles.shape[0]
    groups = lax.axis_size("grp")
    i32 = jnp.int32
    dma = pltpu.SemaphoreType.DMA
    peers = GROUP - 1

    req, slot, table = pl.pallas_call(
        functools.partial(prep_kernel, block_count),
        out_shape=(
            jax.ShapeDtypeStruct((SLOTS,), i32),
            jax.ShapeDtypeStruct((ntouch,), i32),
            jax.ShapeDtypeStruct((RB_DEV * ntouch,), i32),
        ),
        in_specs=[sm()] * 4,
        out_specs=(sm(),) * 3,
        scratch_shapes=[SMEM((GROUP,), i32)],
        name="prep",
    )(touched, home, tile_ray, tile_col)

    got, incoming = pl.pallas_call(
        fetch_kernel,
        out_shape=(
            jax.ShapeDtypeStruct((GROUP, CAP, BLK, BLK), bf16),
            jax.ShapeDtypeStruct((SLOTS,), i32),
        ),
        in_specs=[sm(), vm()],
        out_specs=(vm(), sm()),
        scratch_shapes=[
            VMEM((GROUP, 8, BLK), i32),
            VMEM((GROUP, 8, BLK), i32),
            SMEM((GROUP, 8, BLK), i32),
            VMEM((GROUP, CAP, BLK, BLK), bf16),
            dma((peers,)),
            dma((peers,)),
            dma((peers,)),
            dma((peers,)),
            dma,
        ],
        compiler_params=pltpu.CompilerParams(collective_id=1, has_side_effects=True),
        name="fetch",
    )(req, sketch.reshape(block_count, BLK, BLK))

    out = pl.pallas_call(
        functools.partial(apply_kernel, ntouch),
        out_shape=jax.ShapeDtypeStruct((SLOTS, BLK, BLK), bf16),
        in_specs=[sm(), sm(), hbm(), vm()],
        out_specs=vm(),
        scratch_shapes=[
            VMEM((ntiles + 1, BLK, BLK), bf16),
            VMEM((ntouch * BLK, BLK), bf16),
            VMEM((BLK, RB_DEV * BLK), bf16),
            dma((8,)),
        ],
        compiler_params=pltpu.CompilerParams(vmem_limit_bytes=48 << 20),
        name="apply",
    )(table, slot, tiles, got.reshape(SLOTS, BLK, BLK))

    arrived = pl.pallas_call(
        exchange_kernel,
        out_shape=jax.ShapeDtypeStruct((GROUP, CAP, BLK, BLK), bf16),
        in_specs=[vm()],
        out_specs=vm(),
        scratch_shapes=[dma((peers,)), dma((peers,))],
        compiler_params=pltpu.CompilerParams(collective_id=2, has_side_effects=True),
        name="exchange",
    )(out.reshape(GROUP, CAP, BLK, BLK))

    normal, both = pl.pallas_call(
        gather_kernel,
        out_shape=(
            jax.ShapeDtypeStruct((block_count, BLK, BLK), f32),
            jax.ShapeDtypeStruct((BLK, 2 * BLK), f32),
        ),
        in_specs=[sm(), vm()],
        out_specs=(vm(), vm()),
        name="gather",
    )(incoming, arrived.reshape(SLOTS, BLK, BLK))

    voxels = float(sketch.shape[0] * groups * GROUP)
    total = pl.pallas_call(
        functools.partial(reduce_kernel, voxels),
        out_shape=jax.ShapeDtypeStruct((GROUP, BLK // GROUP, BLK), f32),
        in_specs=[vm()],
        out_specs=vm(),
        scratch_shapes=[
            VMEM((GROUP, BLK // GROUP, BLK), f32),
            VMEM((GROUP, BLK // GROUP, BLK), f32),
            VMEM((BLK // GROUP, BLK), f32),
            VMEM((groups, BLK // GROUP, BLK), f32),
            dma((peers,)),
            dma((peers,)),
            dma((groups - 1,)),
            dma((groups - 1,)),
            dma((peers,)),
            dma((peers,)),
        ],
        compiler_params=pltpu.CompilerParams(collective_id=3, has_side_effects=True),
        name="reduce",
    )(both)

    rows = block_count * BLK
    step = rows // 8
    basis, r_factor = pl.pallas_call(
        basis_kernel,
        grid=(8,),
        out_shape=(
            jax.ShapeDtypeStruct((rows, BLK), f32),
            jax.ShapeDtypeStruct((BLK, BLK), f32),
        ),
        in_specs=[
            pl.BlockSpec((GROUP, BLK // GROUP, BLK), lambda i: (0, 0, 0)),
            pl.BlockSpec((step, BLK), lambda i: (i, 0)),
        ],
        out_specs=(
            pl.BlockSpec((step, BLK), lambda i: (i, 0)),
            pl.BlockSpec((BLK, BLK), lambda i: (0, 0)),
        ),
        scratch_shapes=[VMEM((2 * BLK, 2 * BLK), bf16)],
        name="basis",
    )(total, normal.reshape(rows, BLK))
    return (basis, r_factor)


def solution(mesh):
    in_specs = (
        P(("grp", "dev"), None, None),
        P(("grp", "dev")),
        P(("grp", "dev")),
        P(("grp", "dev")),
        P(),
        P(("grp", "dev"), None),
    )
    out_specs = (P(("grp", "dev"), None), P())
    return jax.shard_map(local, mesh=mesh, in_specs=in_specs, out_specs=out_specs, check_vma=False)
```

```python
import functools

import jax
import jax.numpy as jnp
from jax import lax
from jax.experimental import pallas as pl
from jax.experimental.pallas import tpu as pltpu
from jax.sharding import PartitionSpec as P

CAP = 3
RB_DEV = 32
BLK = 128
SIDE = 4
GROUP = SIDE * SIDE
CHUNKS = 8
SLOTS = GROUP * CAP
gram_shift = 0.001
LEVELS = 32767.0
TINY = 1e-30

MESH = pl.DeviceIdType.MESH
SMEM = pltpu.SMEM
VMEM = pltpu.VMEM
f32 = jnp.float32
bf16 = jnp.bfloat16


def vm():
    return pl.BlockSpec(memory_space=VMEM)


def sm():
    return pl.BlockSpec(memory_space=SMEM)


def hbm():
    return pl.BlockSpec(memory_space=pl.ANY)


OFFSETS = [(dx, dz) for dx in range(SIDE) for dz in range(SIDE) if (dx, dz) != (0, 0)]


def peer_of(me, dx, dz):
    x, z = lax.div(me, SIDE), lax.rem(me, SIDE)
    return lax.rem(x + dx, SIDE) * SIDE + lax.rem(z + dz, SIDE)


def plane_barrier(me):
    barrier = pltpu.get_barrier_semaphore()
    for dx, dz in OFFSETS:
        pl.semaphore_signal(
            barrier, inc=1, device_id={"dev": peer_of(me, dx, dz)}, device_id_type=MESH
        )
    pl.semaphore_wait(barrier, GROUP - 1)


def fetch_kernel(
    block_count,
    touched,
    home,
    sketch_in,
    got,
    incoming,
    slot,
    sketch,
    ask,
    asked,
    asked_s,
    packed,
    send,
    recv,
    asend,
    arecv,
    lsem,
    ssem,
):
    me = lax.axis_index("dev")
    whole = pltpu.make_async_copy(sketch_in, sketch, ssem)
    whole.start()
    barrier = pltpu.get_barrier_semaphore()
    for dx, dz in OFFSETS:
        pl.semaphore_signal(
            barrier, inc=1, device_id={"dev": peer_of(me, dx, dz)}, device_id_type=MESH
        )

    lane = lax.broadcasted_iota(jnp.int32, (8, BLK), 1)
    wanted = jnp.full((8, BLK), -1, jnp.int32)
    holders = []
    for j in range(touched.shape[0]):
        stored = home[touched[j]]
        holder = lax.rem(lax.div(stored, block_count), GROUP)
        n = jnp.int32(0)
        for earlier in holders:
            n = n + (earlier == holder).astype(jnp.int32)
        holders.append(holder)
        s = holder * CAP + n
        slot[j] = s
        wanted = jnp.where(lane == s, lax.rem(stored, block_count), wanted)
    ask[...] = wanted
    asked[me] = wanted

    pl.semaphore_wait(barrier, GROUP - 1)
    asks = []
    for i, (dx, dz) in enumerate(OFFSETS):
        c = pltpu.make_async_remote_copy(
            src_ref=ask,
            dst_ref=asked.at[me],
            send_sem=asend.at[i],
            recv_sem=arecv.at[i],
            device_id={"dev": peer_of(me, dx, dz)},
            device_id_type=MESH,
        )
        c.start()
        asks.append(c)
    whole.wait()
    for c in asks:
        c.wait()
    local = pltpu.make_async_copy(asked, asked_s, lsem)
    local.start()
    local.wait()

    copies = []
    for i, (dx, dz) in enumerate(OFFSETS):
        p = peer_of(me, dx, dz)
        for k in range(CAP):
            packed[p, k] = sketch[jnp.maximum(asked_s[p, 0, CAP * me + k], 0)]
        c = pltpu.make_async_remote_copy(
            src_ref=packed.at[p],
            dst_ref=got.at[me],
            send_sem=send.at[i],
            recv_sem=recv.at[i],
            device_id={"dev": p},
            device_id_type=MESH,
        )
        c.start()
        copies.append(c)
    for k in range(CAP):
        got[me, k] = sketch[jnp.maximum(asked_s[me, 0, CAP * me + k], 0)]
    for p in range(GROUP):
        for k in range(CAP):
            incoming[CAP * p + k] = asked_s[p, 0, CAP * me + k]
    for c in copies:
        c.wait()


def exchange_kernel(out, scales, arrived, arrived_scales, send, recv, send2, recv2):
    me = lax.axis_index("dev")
    plane_barrier(me)
    copies = []
    for i, (dx, dz) in enumerate(OFFSETS):
        p = peer_of(me, dx, dz)
        for src, dst, s, r in (
            (scales, arrived_scales, send2, recv2),
            (out, arrived, send, recv),
        ):
            c = pltpu.make_async_remote_copy(
                src_ref=src.at[p],
                dst_ref=dst.at[me],
                send_sem=s.at[i],
                recv_sem=r.at[i],
                device_id={"dev": p},
                device_id_type=MESH,
            )
            c.start()
            copies.append(c)
    arrived[me] = out[me]
    arrived_scales[me] = scales[me]
    for c in copies:
        c.wait()


def apply_kernel(
    ntouch, ray, col, slot, tiles, xs, out, scales, held, xc, images_t, table, sem
):
    ntiles = tiles.shape[0]
    chunks = 8
    step = ntiles // chunks
    loads = []
    for i in range(chunks):
        c = pltpu.make_async_copy(
            tiles.at[pl.ds(i * step, step)], held.at[pl.ds(i * step, step)], sem.at[i]
        )
        c.start()
        loads.append(c)
    held[ntiles] = jnp.zeros((BLK, BLK), bf16)
    for c in range(ntouch):
        xc[pl.ds(c * BLK, BLK), :] = xs[slot[c]]

    def init(i, c):
        table[i] = ntiles
        return c

    def fill(t, c):
        table[ray[t] * ntouch + col[t]] = t
        return c

    lax.fori_loop(0, RB_DEV * ntouch, init, 0, unroll=16)
    lax.fori_loop(0, ntiles, fill, 0, unroll=16)
    for c in loads:
        c.wait()

    per = 4

    def image_step(g, carry):
        rows = [
            jnp.concatenate(
                [held[table[(g * per + i) * ntouch + c]] for c in range(ntouch)], axis=1
            )
            for i in range(per)
        ]
        lhs = jnp.concatenate(rows, axis=0)
        got = jnp.dot(lhs, xc[...], preferred_element_type=f32)
        start = pl.multiple_of(g * (per * BLK), per * BLK)
        images_t[:, pl.ds(start, per * BLK)] = got.T.astype(bf16)
        return carry

    lax.fori_loop(0, RB_DEV // per, image_step, 0)

    def normal_step(g, carry):
        cols = [
            jnp.concatenate(
                [held[table[r * ntouch + g * 2 + i]] for r in range(RB_DEV)], axis=0
            )
            for i in range(2)
        ]
        rhs = jnp.concatenate(cols, axis=1)
        part = jnp.dot(images_t[...], rhs, preferred_element_type=f32)
        for i in range(2):
            s = slot[g * 2 + i]
            block = part[:, i * BLK : (i + 1) * BLK].T
            top = jnp.maximum(jnp.max(jnp.abs(block), axis=0, keepdims=True), TINY)
            code = jnp.round(block * (LEVELS / top))
            out[s] = code.astype(jnp.int32).astype(jnp.int16)
            scales[lax.div(s, CAP), pl.ds(lax.rem(s, CAP), 1), :] = top * (1.0 / LEVELS)
        return carry

    lax.fori_loop(0, ntouch // 2, normal_step, 0)


def split(value):
    high = value.astype(bf16)
    return high, (value - high.astype(f32)).astype(bf16)


def gather_kernel(incoming, arrived, scales, normal):
    normal[...] = jnp.zeros_like(normal)

    def add(s, c):
        row = incoming[s]

        @pl.when(row >= 0)
        def _():
            scale = scales[lax.div(s, CAP), pl.ds(lax.rem(s, CAP), 1), :]
            code = arrived[s].astype(jnp.int32).astype(f32)
            normal[row] = normal[row] + code * scale

        return c

    lax.fori_loop(0, SLOTS, add, 0)


def reduce_kernel(
    voxels, normal, total, held, both, mine, first, part, second, s1, r1, s2, r2, s3, r3, lsem
):
    me = lax.axis_index("dev")
    grp = lax.axis_index("grp")
    groups = lax.axis_size("grp")
    blocks = held.shape[0]
    per = blocks // CHUNKS
    loads = []
    for i in range(CHUNKS):
        c = pltpu.make_async_copy(
            normal.at[pl.ds(i * per, per)], held.at[pl.ds(i * per, per)], lsem.at[i]
        )
        c.start()
        loads.append(c)

    barrier = pltpu.get_barrier_semaphore()
    for dx, dz in OFFSETS:
        pl.semaphore_signal(
            barrier, inc=1, device_id={"dev": peer_of(me, dx, dz)}, device_id_type=MESH
        )
    for o in range(1, groups):
        pl.semaphore_signal(
            barrier, inc=1, device_id={"grp": lax.rem(grp + o, groups)}, device_id_type=MESH
        )

    both[...] = jnp.zeros_like(both)
    for c in loads:
        c.wait()

    def accumulate(g, c):
        rows = held[pl.ds(g * per, per)].reshape(per * BLK, BLK)
        high, low = split(rows)
        pair = jnp.concatenate([high, low], axis=1)
        both[...] += lax.dot_general(
            high, pair, (((0,), (0,)), ((), ())), preferred_element_type=f32
        )
        return c

    lax.fori_loop(0, CHUNKS, accumulate, 0)
    cross = both[:, BLK:]
    mine[...] = (both[:, :BLK] + cross + cross.T).reshape(mine.shape)
    pl.semaphore_wait(barrier, GROUP - 1 + groups - 1)

    copies = []
    for i, (dx, dz) in enumerate(OFFSETS):
        p = peer_of(me, dx, dz)
        c = pltpu.make_async_remote_copy(
            src_ref=mine.at[p],
            dst_ref=first.at[me],
            send_sem=s1.at[i],
            recv_sem=r1.at[i],
            device_id={"dev": p},
            device_id_type=MESH,
        )
        c.start()
        copies.append(c)
    first[me] = mine[me]
    for c in copies:
        c.wait()
    chunk = first[0]
    for p in range(1, GROUP):
        chunk = chunk + first[p]
    part[...] = chunk

    copies = []
    for o in range(1, groups):
        g = lax.rem(grp + o, groups)
        c = pltpu.make_async_remote_copy(
            src_ref=part,
            dst_ref=second.at[grp],
            send_sem=s2.at[o - 1],
            recv_sem=r2.at[o - 1],
            device_id={"grp": g},
            device_id_type=MESH,
        )
        c.start()
        copies.append(c)
    second[grp] = chunk
    for c in copies:
        c.wait()
    chunk = second[0]
    for g in range(1, groups):
        chunk = chunk + second[g]
    total[me] = chunk / voxels

    copies = []
    for i, (dx, dz) in enumerate(OFFSETS):
        p = peer_of(me, dx, dz)
        c = pltpu.make_async_remote_copy(
            src_ref=total.at[me],
            dst_ref=total.at[me],
            send_sem=s3.at[i],
            recv_sem=r3.at[i],
            device_id={"dev": p},
            device_id_type=MESH,
        )
        c.start()
        copies.append(c)
    for c in copies:
        c.wait()


def factor(gram):
    n = gram.shape[0]
    bands = n // 8
    shape = (8, n)
    row_id = lax.broadcasted_iota(jnp.int32, shape, 0)
    lane_id = lax.broadcasted_iota(jnp.int32, shape, 1)
    g = [gram[8 * b : 8 * b + 8, :] for b in range(bands)]
    w = [jnp.where(lane_id == row_id + 8 * b, 1.0, 0.0).astype(f32) for b in range(bands)]
    r_bands, w_bands = [], []
    for b in range(bands):
        cols = [
            [jnp.broadcast_to(g[t][:, 8 * b + k : 8 * b + k + 1], shape) for k in range(8)]
            for t in range(b, bands)
        ]
        cols[0] = [jnp.where(lane_id < n, c, 0.0) for c in cols[0]]
        pivots = jnp.ones(shape, f32)
        for k in range(8):
            pivot = jnp.broadcast_to(cols[0][k][k : k + 1, :], shape)
            scale = 1.0 / pivot
            pivots = jnp.where(row_id == k, pivot, pivots)
            g_s = jnp.broadcast_to(g[b][k : k + 1, :], shape) * scale
            w_s = jnp.broadcast_to(w[b][k : k + 1, :], shape) * scale
            c_s = {
                j: jnp.broadcast_to(cols[0][j][k : k + 1, :], shape) * scale
                for j in range(k + 1, 8)
            }
            for t in range(b, bands):
                own = cols[t - b]
                f = own[k]
                if t == b:
                    if k == 7:
                        continue
                    f = jnp.where(row_id > k, f, 0.0)
                for j in range(k + 1, 8):
                    own[j] = own[j] - f * c_s[j]
                g[t] = g[t] - f * g_s
                w[t] = w[t] - f * w_s
        root = 1.0 / jnp.sqrt(pivots)
        r_bands.append(jnp.where(lane_id >= row_id + 8 * b, g[b] * root, 0.0))
        w_bands.append(w[b] * root)
    return jnp.concatenate(r_bands, axis=0), jnp.concatenate(w_bands, axis=0)


def basis_kernel(total, normal, basis, r_factor, inverse):
    @pl.when(pl.program_id(0) == 0)
    def _():
        rows = lax.broadcasted_iota(jnp.int32, (BLK, BLK), 0)
        cols = lax.broadcasted_iota(jnp.int32, (BLK, BLK), 1)
        gram = total[...].reshape(BLK, BLK)
        gram = gram + jnp.where(rows == cols, gram_shift, 0.0).astype(f32)
        r_value, lower_inverse = factor(gram)
        r_factor[...] = r_value
        high, low = split(lower_inverse.T)
        inverse[:BLK, :BLK] = high
        inverse[BLK:, :BLK] = high
        inverse[:BLK, BLK:] = low
        inverse[BLK:, BLK:] = jnp.zeros_like(low)

    high, low = split(normal[...])
    got = jnp.dot(
        jnp.concatenate([high, low], axis=1), inverse[...], preferred_element_type=f32
    )
    basis[...] = got[:, :BLK] + got[:, BLK:]


def local(tiles, tile_ray, tile_col, touched, home, sketch):
    block_count = sketch.shape[0] // BLK
    ntouch = touched.shape[0]
    ntiles = tiles.shape[0]
    groups = lax.axis_size("grp")
    i32 = jnp.int32
    dma = pltpu.SemaphoreType.DMA
    peers = GROUP - 1

    got, incoming, slot = pl.pallas_call(
        functools.partial(fetch_kernel, block_count),
        out_shape=(
            jax.ShapeDtypeStruct((GROUP, CAP, BLK, BLK), bf16),
            jax.ShapeDtypeStruct((SLOTS,), i32),
            jax.ShapeDtypeStruct((ntouch,), i32),
        ),
        in_specs=[sm(), sm(), hbm()],
        out_specs=(vm(), sm(), sm()),
        scratch_shapes=[
            VMEM((block_count, BLK, BLK), bf16),
            VMEM((8, BLK), i32),
            VMEM((GROUP, 8, BLK), i32),
            SMEM((GROUP, 8, BLK), i32),
            VMEM((GROUP, CAP, BLK, BLK), bf16),
            dma((peers,)),
            dma((peers,)),
            dma((peers,)),
            dma((peers,)),
            dma,
            dma,
        ],
        compiler_params=pltpu.CompilerParams(collective_id=1, has_side_effects=True),
        name="fetch",
    )(touched, home, sketch.reshape(block_count, BLK, BLK))

    out, scales = pl.pallas_call(
        functools.partial(apply_kernel, ntouch),
        out_shape=(
            jax.ShapeDtypeStruct((SLOTS, BLK, BLK), jnp.int16),
            jax.ShapeDtypeStruct((GROUP, 8, BLK), f32),
        ),
        in_specs=[sm(), sm(), sm(), hbm(), vm()],
        out_specs=(vm(), vm()),
        scratch_shapes=[
            VMEM((ntiles + 1, BLK, BLK), bf16),
            VMEM((ntouch * BLK, BLK), bf16),
            VMEM((BLK, RB_DEV * BLK), bf16),
            SMEM((RB_DEV * ntouch,), i32),
            dma((8,)),
        ],
        compiler_params=pltpu.CompilerParams(vmem_limit_bytes=48 << 20),
        name="apply",
    )(tile_ray, tile_col, slot, tiles, got.reshape(SLOTS, BLK, BLK))

    arrived, arrived_scales = pl.pallas_call(
        exchange_kernel,
        out_shape=(
            jax.ShapeDtypeStruct((GROUP, CAP, BLK, BLK), jnp.int16),
            jax.ShapeDtypeStruct((GROUP, 8, BLK), f32),
        ),
        in_specs=[vm(), vm()],
        out_specs=(vm(), vm()),
        scratch_shapes=[dma((peers,))] * 4,
        compiler_params=pltpu.CompilerParams(collective_id=2, has_side_effects=True),
        name="exchange",
    )(out.reshape(GROUP, CAP, BLK, BLK), scales)

    normal = pl.pallas_call(
        gather_kernel,
        out_shape=jax.ShapeDtypeStruct((block_count, BLK, BLK), f32),
        in_specs=[sm(), vm(), vm()],
        out_specs=vm(),
        name="gather",
    )(incoming, arrived.reshape(SLOTS, BLK, BLK), arrived_scales)

    voxels = float(sketch.shape[0] * groups * GROUP)
    total = pl.pallas_call(
        functools.partial(reduce_kernel, voxels),
        out_shape=jax.ShapeDtypeStruct((GROUP, BLK // GROUP, BLK), f32),
        in_specs=[hbm()],
        out_specs=vm(),
        scratch_shapes=[
            VMEM((block_count, BLK, BLK), f32),
            VMEM((BLK, 2 * BLK), f32),
            VMEM((GROUP, BLK // GROUP, BLK), f32),
            VMEM((GROUP, BLK // GROUP, BLK), f32),
            VMEM((BLK // GROUP, BLK), f32),
            VMEM((groups, BLK // GROUP, BLK), f32),
            dma((peers,)),
            dma((peers,)),
            dma((groups - 1,)),
            dma((groups - 1,)),
            dma((peers,)),
            dma((peers,)),
            dma((CHUNKS,)),
        ],
        compiler_params=pltpu.CompilerParams(collective_id=3, has_side_effects=True),
        name="reduce",
    )(normal)

    rows = block_count * BLK
    step = rows // 8
    basis, r_factor = pl.pallas_call(
        basis_kernel,
        grid=(8,),
        out_shape=(
            jax.ShapeDtypeStruct((rows, BLK), f32),
            jax.ShapeDtypeStruct((BLK, BLK), f32),
        ),
        in_specs=[
            pl.BlockSpec((GROUP, BLK // GROUP, BLK), lambda i: (0, 0, 0)),
            pl.BlockSpec((step, BLK), lambda i: (i, 0)),
        ],
        out_specs=(
            pl.BlockSpec((step, BLK), lambda i: (i, 0)),
            pl.BlockSpec((BLK, BLK), lambda i: (0, 0)),
        ),
        scratch_shapes=[VMEM((2 * BLK, 2 * BLK), bf16)],
        name="basis",
    )(total, normal.reshape(rows, BLK))
    return (basis, r_factor)


def solution(mesh):
    in_specs = (
        P(("grp", "dev"), None, None),
        P(("grp", "dev")),
        P(("grp", "dev")),
        P(("grp", "dev")),
        P(),
        P(("grp", "dev"), None),
    )
    out_specs = (P(("grp", "dev"), None), P())
    return jax.shard_map(local, mesh=mesh, in_specs=in_specs, out_specs=out_specs, check_vma=False)
```

```python
import functools

import jax
import jax.numpy as jnp
from jax import lax
from jax.experimental import pallas as pl
from jax.experimental.pallas import tpu as pltpu
from jax.sharding import PartitionSpec as P

CAP = 3
RB_DEV = 32
BLK = 128
SIDE = 4
GROUP = SIDE * SIDE
CHUNKS = 8
PER = 8
SLOTS = GROUP * CAP
gram_shift = 0.001
LEVELS = 32767.0
TINY = 1e-30

MESH = pl.DeviceIdType.MESH
SMEM = pltpu.SMEM
VMEM = pltpu.VMEM
f32 = jnp.float32
bf16 = jnp.bfloat16


def vm():
    return pl.BlockSpec(memory_space=VMEM)


def sm():
    return pl.BlockSpec(memory_space=SMEM)


def hbm():
    return pl.BlockSpec(memory_space=pl.ANY)


OFFSETS = sorted(
    [(dx, dz) for dx in range(SIDE) for dz in range(SIDE) if (dx, dz) != (0, 0)],
    key=lambda o: (-(min(o[0], SIDE - o[0]) + min(o[1], SIDE - o[1])), o),
)


def peer_of(me, dx, dz):
    x, z = lax.div(me, SIDE), lax.rem(me, SIDE)
    return lax.rem(x + dx, SIDE) * SIDE + lax.rem(z + dz, SIDE)


def cycle_kernel(
    block_count,
    touched,
    home,
    ray,
    col,
    sketch_in,
    tiles_in,
    arrived,
    arrived_scales,
    incoming,
    sketch,
    held,
    ask,
    asked,
    asked_s,
    index,
    index_s,
    place_s,
    packed,
    got,
    xc,
    images_t,
    codes,
    code_scales,
    out,
    scales,
    asend,
    arecv,
    send,
    recv,
    send2,
    recv2,
    send3,
    recv3,
    tsem,
    ssem,
    lsem,
    isem,
):
    me = lax.axis_index("dev")
    ntouch = touched.shape[0]
    ntiles = ray.shape[0]
    i32 = jnp.int32
    whole = pltpu.make_async_copy(sketch_in, sketch, ssem)
    whole.start()
    step = ntiles // CHUNKS
    loads = []
    for i in range(CHUNKS):
        c = pltpu.make_async_copy(
            tiles_in.at[pl.ds(i * step, step)], held.at[pl.ds(i * step, step)], tsem.at[i]
        )
        c.start()
        loads.append(c)
    barrier = pltpu.get_barrier_semaphore()
    for dx, dz in OFFSETS:
        pl.semaphore_signal(
            barrier, inc=1, device_id={"dev": peer_of(me, dx, dz)}, device_id_type=MESH
        )

    for q, (dx, dz) in enumerate(OFFSETS + [(0, 0)]):
        place_s[dx * SIDE + dz] = q
    x, z = lax.div(me, SIDE), lax.rem(me, SIDE)
    lane = lax.broadcasted_iota(i32, (8, BLK), 1)
    row = lax.broadcasted_iota(i32, (8, BLK), 0)
    wanted = jnp.full((8, BLK), -1, i32)
    holders, slots, keys = [], [], []
    for j in range(ntouch):
        stored = home[touched[j]]
        holder = lax.rem(lax.div(stored, block_count), GROUP)
        n = i32(0)
        for earlier in holders:
            n = n + (earlier == holder).astype(i32)
        n = jnp.minimum(n, CAP - 1)
        holders.append(holder)
        s = holder * CAP + n
        slots.append(s)
        hx, hz = lax.div(holder, SIDE), lax.rem(holder, SIDE)
        far = lax.rem(hx - x + SIDE, SIDE) * SIDE + lax.rem(hz - z + SIDE, SIDE)
        keys.append(place_s[far] * CAP + n)
        wanted = jnp.where(lane == s, lax.rem(stored, block_count), wanted)
    ask[...] = wanted
    asked[me] = wanted

    pl.semaphore_wait(barrier, GROUP - 1)
    asks = []
    for i, (dx, dz) in enumerate(OFFSETS):
        c = pltpu.make_async_remote_copy(
            src_ref=ask,
            dst_ref=asked.at[me],
            send_sem=asend.at[i],
            recv_sem=arecv.at[i],
            device_id={"dev": peer_of(me, dx, dz)},
            device_id_type=MESH,
        )
        c.start()
        asks.append(c)

    order = jnp.zeros((8, BLK), i32)
    for j in range(ntouch):
        rank = i32(0)
        for k in range(ntouch):
            if k != j:
                rank = rank + (keys[k] < keys[j]).astype(i32)
        order = jnp.where((row == 0) & (lane == rank), j, order)
        order = jnp.where((row == 1) & (lane == keys[j]), rank, order)
    index[pl.ds(RB_DEV, 8), :] = order

    bands = RB_DEV // 8
    pairs = [
        jnp.where(lane < ntouch, (row + 8 * b) * ntouch + lane, -1) for b in range(bands)
    ]

    def place(t, table):
        pair = ray[t] * ntouch + col[t]
        return tuple(jnp.where(p == pair, t, v) for p, v in zip(pairs, table))

    table = lax.fori_loop(
        0, ntiles, place, (jnp.full((8, BLK), ntiles, i32),) * bands, unroll=8
    )
    for b in range(bands):
        index[pl.ds(8 * b, 8), :] = table[b]
    tables = pltpu.make_async_copy(index, index_s, isem)
    tables.start()
    held[ntiles] = jnp.zeros((BLK, BLK), bf16)

    whole.wait()
    for c in asks:
        c.wait()
    local = pltpu.make_async_copy(asked, asked_s, lsem)
    local.start()
    local.wait()

    copies = []
    for i, (dx, dz) in enumerate(OFFSETS):
        p = peer_of(me, dx, dz)
        for k in range(CAP):
            packed[p, k] = sketch[jnp.maximum(asked_s[p, 0, CAP * me + k], 0)]
        c = pltpu.make_async_remote_copy(
            src_ref=packed.at[p],
            dst_ref=got.at[me],
            send_sem=send.at[i],
            recv_sem=recv.at[i],
            device_id={"dev": p},
            device_id_type=MESH,
        )
        c.start()
        copies.append(c)
    for k in range(CAP):
        got[me, k] = sketch[jnp.maximum(asked_s[me, 0, CAP * me + k], 0)]
    for p in range(GROUP):
        for k in range(CAP):
            incoming[CAP * p + k] = asked_s[p, 0, CAP * me + k]
    tables.wait()
    for c in loads:
        c.wait()
    for c in copies:
        c.wait()

    for c in range(ntouch):
        holder = holders[c]
        xc[pl.ds(c * BLK, BLK), :] = got[holder, slots[c] - CAP * holder]

    def image_step(g, carry):
        rows = [
            jnp.concatenate(
                [held[index_s[g * PER + i, c]] for c in range(ntouch)], axis=1
            )
            for i in range(PER)
        ]
        lhs = jnp.concatenate(rows, axis=0)
        image = jnp.dot(lhs, xc[...], preferred_element_type=f32)
        start = pl.multiple_of(g * (PER * BLK), PER * BLK)
        images_t[:, pl.ds(start, PER * BLK)] = image.T.astype(bf16)
        return carry

    lax.fori_loop(0, RB_DEV // PER, image_step, 0)

    def normal_step(g, carry):
        cols = []
        for i in range(2):
            c = index_s[RB_DEV, 2 * g + i]
            cols.append(
                jnp.concatenate([held[index_s[r, c]] for r in range(RB_DEV)], axis=0)
            )
        rhs = jnp.concatenate(cols, axis=1)
        part = jnp.dot(images_t[...], rhs, preferred_element_type=f32)
        for i in range(2):
            block = part[:, i * BLK : (i + 1) * BLK].T
            top = jnp.maximum(jnp.max(jnp.abs(block), axis=0, keepdims=True), TINY)
            code = jnp.round(block * (LEVELS / top))
            codes[2 * g + i] = code.astype(i32).astype(jnp.int16)
            code_scales[pl.ds(2 * g + i, 1), :] = top * (1.0 / LEVELS)
        return carry

    copies = []
    done = 0
    for q in range(GROUP - 1):
        until = -(-min(ntouch, CAP * (q + 1)) // 2)
        if until > done:
            lax.fori_loop(done, until, normal_step, 0)
            done = until
        p = peer_of(me, *OFFSETS[q])
        for k in range(CAP):
            at = index_s[RB_DEV + 1, CAP * q + k]
            out[p, k] = codes[at]
            scales[p, pl.ds(k, 1), :] = code_scales[pl.ds(at, 1), :]
        for src, dst, ss, rs in (
            (scales, arrived_scales, send2, recv2),
            (out, arrived, send3, recv3),
        ):
            c = pltpu.make_async_remote_copy(
                src_ref=src.at[p],
                dst_ref=dst.at[me],
                send_sem=ss.at[q],
                recv_sem=rs.at[q],
                device_id={"dev": p},
                device_id_type=MESH,
            )
            c.start()
            copies.append(c)
    for k in range(CAP):
        at = index_s[RB_DEV + 1, CAP * (GROUP - 1) + k]
        arrived[me, k] = codes[at]
        arrived_scales[me, pl.ds(k, 1), :] = code_scales[pl.ds(at, 1), :]
    for c in copies:
        c.wait()


def split(value):
    high = value.astype(bf16)
    return high, (value - high.astype(f32)).astype(bf16)


def gather_kernel(incoming, arrived, scales, normal):
    normal[...] = jnp.zeros_like(normal)

    def add(s, c):
        row = incoming[s]

        @pl.when(row >= 0)
        def _():
            scale = scales[lax.div(s, CAP), pl.ds(lax.rem(s, CAP), 1), :]
            code = arrived[s].astype(jnp.int32).astype(f32)
            normal[row] = normal[row] + code * scale

        return c

    lax.fori_loop(0, SLOTS, add, 0)


def reduce_kernel(
    voxels, normal, total, held, both, mine, first, part, second, s1, r1, s2, r2, s3, r3, lsem
):
    me = lax.axis_index("dev")
    grp = lax.axis_index("grp")
    groups = lax.axis_size("grp")
    blocks = held.shape[0]
    per = blocks // CHUNKS
    loads = []
    for i in range(CHUNKS):
        c = pltpu.make_async_copy(
            normal.at[pl.ds(i * per, per)], held.at[pl.ds(i * per, per)], lsem.at[i]
        )
        c.start()
        loads.append(c)

    barrier = pltpu.get_barrier_semaphore()
    for dx, dz in OFFSETS:
        pl.semaphore_signal(
            barrier, inc=1, device_id={"dev": peer_of(me, dx, dz)}, device_id_type=MESH
        )
    for o in range(1, groups):
        pl.semaphore_signal(
            barrier, inc=1, device_id={"grp": lax.rem(grp + o, groups)}, device_id_type=MESH
        )

    both[...] = jnp.zeros_like(both)
    for c in loads:
        c.wait()

    def accumulate(g, c):
        rows = held[pl.ds(g * per, per)].reshape(per * BLK, BLK)
        high, low = split(rows)
        pair = jnp.concatenate([high, low], axis=1)
        both[...] += lax.dot_general(
            high, pair, (((0,), (0,)), ((), ())), preferred_element_type=f32
        )
        return c

    lax.fori_loop(0, CHUNKS, accumulate, 0)
    cross = both[:, BLK:]
    mine[...] = (both[:, :BLK] + cross + cross.T).reshape(mine.shape)
    pl.semaphore_wait(barrier, GROUP - 1 + groups - 1)

    copies = []
    for i, (dx, dz) in enumerate(OFFSETS):
        p = peer_of(me, dx, dz)
        c = pltpu.make_async_remote_copy(
            src_ref=mine.at[p],
            dst_ref=first.at[me],
            send_sem=s1.at[i],
            recv_sem=r1.at[i],
            device_id={"dev": p},
            device_id_type=MESH,
        )
        c.start()
        copies.append(c)
    first[me] = mine[me]
    for c in copies:
        c.wait()
    chunk = first[0]
    for p in range(1, GROUP):
        chunk = chunk + first[p]
    part[...] = chunk

    copies = []
    for o in range(1, groups):
        g = lax.rem(grp + o, groups)
        c = pltpu.make_async_remote_copy(
            src_ref=part,
            dst_ref=second.at[grp],
            send_sem=s2.at[o - 1],
            recv_sem=r2.at[o - 1],
            device_id={"grp": g},
            device_id_type=MESH,
        )
        c.start()
        copies.append(c)
    second[grp] = chunk
    for c in copies:
        c.wait()
    chunk = second[0]
    for g in range(1, groups):
        chunk = chunk + second[g]
    total[me] = chunk / voxels

    copies = []
    for i, (dx, dz) in enumerate(OFFSETS):
        p = peer_of(me, dx, dz)
        c = pltpu.make_async_remote_copy(
            src_ref=total.at[me],
            dst_ref=total.at[me],
            send_sem=s3.at[i],
            recv_sem=r3.at[i],
            device_id={"dev": p},
            device_id_type=MESH,
        )
        c.start()
        copies.append(c)
    for c in copies:
        c.wait()


def factor(gram):
    n = gram.shape[0]
    bands = n // 8
    shape = (8, n)
    row_id = lax.broadcasted_iota(jnp.int32, shape, 0)
    lane_id = lax.broadcasted_iota(jnp.int32, shape, 1)
    g = [gram[8 * b : 8 * b + 8, :] for b in range(bands)]
    w = [jnp.where(lane_id == row_id + 8 * b, 1.0, 0.0).astype(f32) for b in range(bands)]
    r_bands, w_bands = [], []
    for b in range(bands):
        cols = [
            [jnp.broadcast_to(g[t][:, 8 * b + k : 8 * b + k + 1], shape) for k in range(8)]
            for t in range(b, bands)
        ]
        cols[0] = [jnp.where(lane_id < n, c, 0.0) for c in cols[0]]
        pivots = jnp.ones(shape, f32)
        for k in range(8):
            pivot = jnp.broadcast_to(cols[0][k][k : k + 1, :], shape)
            scale = 1.0 / pivot
            pivots = jnp.where(row_id == k, pivot, pivots)
            g_s = jnp.broadcast_to(g[b][k : k + 1, :], shape) * scale
            w_s = jnp.broadcast_to(w[b][k : k + 1, :], shape) * scale
            c_s = {
                j: jnp.broadcast_to(cols[0][j][k : k + 1, :], shape) * scale
                for j in range(k + 1, 8)
            }
            for t in range(b, bands):
                own = cols[t - b]
                f = own[k]
                if t == b:
                    if k == 7:
                        continue
                    f = jnp.where(row_id > k, f, 0.0)
                for j in range(k + 1, 8):
                    own[j] = own[j] - f * c_s[j]
                g[t] = g[t] - f * g_s
                w[t] = w[t] - f * w_s
        root = 1.0 / jnp.sqrt(pivots)
        r_bands.append(jnp.where(lane_id >= row_id + 8 * b, g[b] * root, 0.0))
        w_bands.append(w[b] * root)
    return jnp.concatenate(r_bands, axis=0), jnp.concatenate(w_bands, axis=0)


def basis_kernel(total, normal, basis, r_factor, inverse):
    @pl.when(pl.program_id(0) == 0)
    def _():
        rows = lax.broadcasted_iota(jnp.int32, (BLK, BLK), 0)
        cols = lax.broadcasted_iota(jnp.int32, (BLK, BLK), 1)
        gram = total[...].reshape(BLK, BLK)
        gram = gram + jnp.where(rows == cols, gram_shift, 0.0).astype(f32)
        r_value, lower_inverse = factor(gram)
        r_factor[...] = r_value
        high, low = split(lower_inverse.T)
        inverse[:BLK, :BLK] = high
        inverse[BLK:, :BLK] = high
        inverse[:BLK, BLK:] = low
        inverse[BLK:, BLK:] = jnp.zeros_like(low)

    high, low = split(normal[...])
    got = jnp.dot(
        jnp.concatenate([high, low], axis=1), inverse[...], preferred_element_type=f32
    )
    basis[...] = got[:, :BLK] + got[:, BLK:]


def local(tiles, tile_ray, tile_col, touched, home, sketch):
    block_count = sketch.shape[0] // BLK
    ntouch = touched.shape[0]
    ntiles = tiles.shape[0]
    groups = lax.axis_size("grp")
    i32 = jnp.int32
    dma = pltpu.SemaphoreType.DMA
    peers = GROUP - 1

    arrived, arrived_scales, incoming = pl.pallas_call(
        functools.partial(cycle_kernel, block_count),
        out_shape=(
            jax.ShapeDtypeStruct((GROUP, CAP, BLK, BLK), jnp.int16),
            jax.ShapeDtypeStruct((GROUP, 8, BLK), f32),
            jax.ShapeDtypeStruct((SLOTS,), i32),
        ),
        in_specs=[sm(), sm(), sm(), sm(), hbm(), hbm()],
        out_specs=(vm(), vm(), sm()),
        scratch_shapes=[
            VMEM((block_count, BLK, BLK), bf16),
            VMEM((ntiles + 1, BLK, BLK), bf16),
            VMEM((8, BLK), i32),
            VMEM((GROUP, 8, BLK), i32),
            SMEM((GROUP, 8, BLK), i32),
            VMEM((RB_DEV + 8, BLK), i32),
            SMEM((RB_DEV + 8, BLK), i32),
            SMEM((GROUP,), i32),
            VMEM((GROUP, CAP, BLK, BLK), bf16),
            VMEM((GROUP, CAP, BLK, BLK), bf16),
            VMEM((ntouch * BLK, BLK), bf16),
            VMEM((BLK, RB_DEV * BLK), bf16),
            VMEM((ntouch, BLK, BLK), jnp.int16),
            VMEM((ntouch, BLK), f32),
            VMEM((GROUP, CAP, BLK, BLK), jnp.int16),
            VMEM((GROUP, 8, BLK), f32),
        ]
        + [dma((peers,))] * 8
        + [dma((CHUNKS,)), dma, dma, dma],
        compiler_params=pltpu.CompilerParams(collective_id=1, has_side_effects=True),
        name="cycle",
    )(touched, home, tile_ray, tile_col, sketch.reshape(block_count, BLK, BLK), tiles)

    normal = pl.pallas_call(
        gather_kernel,
        out_shape=jax.ShapeDtypeStruct((block_count, BLK, BLK), f32),
        in_specs=[sm(), vm(), vm()],
        out_specs=vm(),
        name="gather",
    )(incoming, arrived.reshape(SLOTS, BLK, BLK), arrived_scales)

    voxels = float(sketch.shape[0] * groups * GROUP)
    total = pl.pallas_call(
        functools.partial(reduce_kernel, voxels),
        out_shape=jax.ShapeDtypeStruct((GROUP, BLK // GROUP, BLK), f32),
        in_specs=[hbm()],
        out_specs=vm(),
        scratch_shapes=[
            VMEM((block_count, BLK, BLK), f32),
            VMEM((BLK, 2 * BLK), f32),
            VMEM((GROUP, BLK // GROUP, BLK), f32),
            VMEM((GROUP, BLK // GROUP, BLK), f32),
            VMEM((BLK // GROUP, BLK), f32),
            VMEM((groups, BLK // GROUP, BLK), f32),
            dma((peers,)),
            dma((peers,)),
            dma((groups - 1,)),
            dma((groups - 1,)),
            dma((peers,)),
            dma((peers,)),
            dma((CHUNKS,)),
        ],
        compiler_params=pltpu.CompilerParams(collective_id=3, has_side_effects=True),
        name="reduce",
    )(normal)

    rows = block_count * BLK
    step = rows // 8
    basis, r_factor = pl.pallas_call(
        basis_kernel,
        grid=(8,),
        out_shape=(
            jax.ShapeDtypeStruct((rows, BLK), f32),
            jax.ShapeDtypeStruct((BLK, BLK), f32),
        ),
        in_specs=[
            pl.BlockSpec((GROUP, BLK // GROUP, BLK), lambda i: (0, 0, 0)),
            pl.BlockSpec((step, BLK), lambda i: (i, 0)),
        ],
        out_specs=(
            pl.BlockSpec((step, BLK), lambda i: (i, 0)),
            pl.BlockSpec((BLK, BLK), lambda i: (0, 0)),
        ),
        scratch_shapes=[VMEM((2 * BLK, 2 * BLK), bf16)],
        name="basis",
    )(total, normal.reshape(rows, BLK))
    return (basis, r_factor)


def solution(mesh):
    in_specs = (
        P(("grp", "dev"), None, None),
        P(("grp", "dev")),
        P(("grp", "dev")),
        P(("grp", "dev")),
        P(),
        P(("grp", "dev"), None),
    )
    out_specs = (P(("grp", "dev"), None), P())
    return jax.shard_map(local, mesh=mesh, in_specs=in_specs, out_specs=out_specs, check_vma=False)
```

```python
import functools

import jax
import jax.numpy as jnp
from jax import lax
from jax.experimental import pallas as pl
from jax.experimental.pallas import tpu as pltpu
from jax.sharding import PartitionSpec as P

CAP = 3
RB_DEV = 32
BLK = 128
SIDE = 4
GROUP = SIDE * SIDE
CHUNKS = 8
PER = 8
STAGES = (12, 14, 16)
ORDER = RB_DEV
PLACE = RB_DEV + 1
COMING = RB_DEV + 2
SLOT = RB_DEV + 3
SLOTS = GROUP * CAP
gram_shift = 0.001
LEVELS = 32767.0
TINY = 1e-30

MESH = pl.DeviceIdType.MESH
SMEM = pltpu.SMEM
VMEM = pltpu.VMEM
f32 = jnp.float32
bf16 = jnp.bfloat16


def vm():
    return pl.BlockSpec(memory_space=VMEM)


def sm():
    return pl.BlockSpec(memory_space=SMEM)


def hbm():
    return pl.BlockSpec(memory_space=pl.ANY)


OFFSETS = sorted(
    [(dx, dz) for dx in range(SIDE) for dz in range(SIDE) if (dx, dz) != (0, 0)],
    key=lambda o: (-(min(o[0], SIDE - o[0]) + min(o[1], SIDE - o[1])), o),
)


def peer_of(me, dx, dz):
    x, z = lax.div(me, SIDE), lax.rem(me, SIDE)
    return lax.rem(x + dx, SIDE) * SIDE + lax.rem(z + dz, SIDE)


def cycle_kernel(
    block_count,
    touched,
    home,
    ray,
    col,
    sketch_in,
    tiles_in,
    arrived,
    arrived_scales,
    incoming,
    sketch,
    held,
    ask,
    asked,
    asked_s,
    index,
    index_s,
    place_s,
    coming_s,
    packed,
    got_0,
    got_1,
    got_2,
    xc,
    sums,
    images_t,
    codes,
    code_scales,
    out,
    scales,
    asend,
    arecv,
    send,
    recv,
    send2,
    recv2,
    send3,
    recv3,
    tsem,
    ssem,
    lsem,
    isem,
):
    me = lax.axis_index("dev")
    ntouch = touched.shape[0]
    ntiles = ray.shape[0]
    i32 = jnp.int32
    whole = pltpu.make_async_copy(sketch_in, sketch, ssem)
    whole.start()
    step = ntiles // CHUNKS
    loads = []
    for i in range(CHUNKS):
        c = pltpu.make_async_copy(
            tiles_in.at[pl.ds(i * step, step)], held.at[pl.ds(i * step, step)], tsem.at[i]
        )
        c.start()
        loads.append(c)
    barrier = pltpu.get_barrier_semaphore()
    for dx, dz in OFFSETS:
        pl.semaphore_signal(
            barrier, inc=1, device_id={"dev": peer_of(me, dx, dz)}, device_id_type=MESH
        )

    for q, (dx, dz) in enumerate(OFFSETS + [(0, 0)]):
        place_s[dx * SIDE + dz] = q
        back = (SIDE - dx) % SIDE * SIDE + (SIDE - dz) % SIDE
        coming_s[back] = (q + 1) % GROUP
    x, z = lax.div(me, SIDE), lax.rem(me, SIDE)
    lane = lax.broadcasted_iota(i32, (8, BLK), 1)
    row = lax.broadcasted_iota(i32, (8, BLK), 0)
    wanted = jnp.full((8, BLK), -1, i32)
    holders, keys, arrivals = [], [], []
    for j in range(ntouch):
        stored = home[touched[j]]
        holder = lax.rem(lax.div(stored, block_count), GROUP)
        n = i32(0)
        for earlier in holders:
            n = n + (earlier == holder).astype(i32)
        n = jnp.minimum(n, CAP - 1)
        holders.append(holder)
        s = holder * CAP + n
        hx, hz = lax.div(holder, SIDE), lax.rem(holder, SIDE)
        far = lax.rem(hx - x + SIDE, SIDE) * SIDE + lax.rem(hz - z + SIDE, SIDE)
        keys.append(place_s[far] * CAP + n)
        arrivals.append(coming_s[far] * CAP + n)
        wanted = jnp.where(lane == s, lax.rem(stored, block_count), wanted)
    ask[...] = wanted
    asked[me] = wanted

    pl.semaphore_wait(barrier, GROUP - 1)
    asks = []
    for i, (dx, dz) in enumerate(OFFSETS):
        c = pltpu.make_async_remote_copy(
            src_ref=ask,
            dst_ref=asked.at[me],
            send_sem=asend.at[i],
            recv_sem=arecv.at[i],
            device_id={"dev": peer_of(me, dx, dz)},
            device_id_type=MESH,
        )
        c.start()
        asks.append(c)

    order = jnp.zeros((8, BLK), i32)
    for j in range(ntouch):
        rank = i32(0)
        for k in range(ntouch):
            if k != j:
                rank = rank + (keys[k] < keys[j]).astype(i32)
        order = jnp.where((row == 0) & (lane == rank), j, order)
        order = jnp.where((row == 1) & (lane == keys[j]), rank, order)
        rank = i32(0)
        for k in range(ntouch):
            if k != j:
                rank = rank + (arrivals[k] < arrivals[j]).astype(i32)
        order = jnp.where((row == 2) & (lane == rank), j, order)
        order = jnp.where((row == 3) & (lane == j), arrivals[j], order)
    index[pl.ds(RB_DEV, 8), :] = order

    bands = RB_DEV // 8
    pairs = [
        jnp.where(lane < ntouch, (row + 8 * b) * ntouch + lane, -1) for b in range(bands)
    ]

    def place(t, table):
        pair = ray[t] * ntouch + col[t]
        return tuple(jnp.where(p == pair, t, v) for p, v in zip(pairs, table))

    table = lax.fori_loop(
        0, ntiles, place, (jnp.full((8, BLK), ntiles, i32),) * bands, unroll=8
    )
    for b in range(bands):
        index[pl.ds(8 * b, 8), :] = table[b]
    tables = pltpu.make_async_copy(index, index_s, isem)
    tables.start()
    held[ntiles] = jnp.zeros((BLK, BLK), bf16)

    whole.wait()
    for c in asks:
        c.wait()
    local = pltpu.make_async_copy(asked, asked_s, lsem)
    local.start()
    local.wait()

    got = (got_0, got_1, got_2)
    copies = []
    for i, (dx, dz) in enumerate(OFFSETS):
        p = peer_of(me, dx, dz)
        stage = sum(i + 1 >= owners for owners in STAGES)
        first = (0, *STAGES)[stage]
        for k in range(CAP):
            packed[p, k] = sketch[jnp.maximum(asked_s[p, 0, CAP * me + k], 0)]
        c = pltpu.make_async_remote_copy(
            src_ref=packed.at[p],
            dst_ref=got[stage].at[pl.ds(CAP * (i + 1 - first), CAP)],
            send_sem=send.at[i],
            recv_sem=recv.at[i],
            device_id={"dev": p},
            device_id_type=MESH,
        )
        c.start()
        copies.append(c)
    for k in range(CAP):
        got_0[k] = sketch[jnp.maximum(asked_s[me, 0, CAP * me + k], 0)]
    for p in range(GROUP):
        for k in range(CAP):
            incoming[CAP * p + k] = asked_s[p, 0, CAP * me + k]
    tables.wait()
    for c in loads:
        c.wait()

    received = 0
    begin = 0
    for owners in STAGES:
        for c in copies[received : owners - 1]:
            c.wait_recv()
        received = owners - 1
        end = max(begin, CAP * owners - (SLOTS - ntouch))
        cols = [index_s[COMING, i] for i in range(begin, end)]
        for i, c in enumerate(cols):
            at = index_s[SLOT, c]
            block = got_0[jnp.minimum(at, CAP * STAGES[0] - 1)]
            for stage in range(1, len(STAGES)):
                if STAGES[stage] <= owners:
                    low, high = CAP * STAGES[stage - 1], CAP * STAGES[stage]
                    later = got[stage][jnp.clip(at - low, 0, high - low - 1)]
                    block = jnp.where(at >= low, later, block)
            xc[pl.ds((begin + i) * BLK, BLK), :] = block

        def image_step(g, carry, cols=cols, begin=begin, end=end, last=owners == GROUP):
            rows = [
                jnp.concatenate([held[index_s[g * PER + i, c]] for c in cols], axis=1)
                for i in range(PER)
            ]
            lhs = jnp.concatenate(rows, axis=0)
            known = xc[pl.ds(begin * BLK, (end - begin) * BLK), :]
            image = jnp.dot(lhs, known, preferred_element_type=f32)
            start = pl.multiple_of(g * (PER * BLK), PER * BLK)
            if begin > 0:
                image = image + sums[pl.ds(start, PER * BLK), :]
            if last:
                images_t[:, pl.ds(start, PER * BLK)] = image.T.astype(bf16)
            else:
                sums[pl.ds(start, PER * BLK), :] = image
            return carry

        lax.fori_loop(0, RB_DEV // PER, image_step, 0)
        begin = end
    for c in copies:
        c.wait_send()

    def normal_step(g, carry):
        cols = []
        for i in range(2):
            c = index_s[ORDER, 2 * g + i]
            cols.append(
                jnp.concatenate([held[index_s[r, c]] for r in range(RB_DEV)], axis=0)
            )
        rhs = jnp.concatenate(cols, axis=1)
        part = jnp.dot(images_t[...], rhs, preferred_element_type=f32)
        for i in range(2):
            block = part[:, i * BLK : (i + 1) * BLK].T
            top = jnp.maximum(jnp.max(jnp.abs(block), axis=0, keepdims=True), TINY)
            code = jnp.round(block * (LEVELS / top))
            codes[2 * g + i] = code.astype(i32).astype(jnp.int16)
            code_scales[pl.ds(2 * g + i, 1), :] = top * (1.0 / LEVELS)
        return carry

    copies = []
    done = 0
    for q in range(GROUP - 1):
        until = -(-min(ntouch, CAP * (q + 1)) // 2)
        if until > done:
            lax.fori_loop(done, until, normal_step, 0)
            done = until
        p = peer_of(me, *OFFSETS[q])
        for k in range(CAP):
            at = index_s[PLACE, CAP * q + k]
            out[p, k] = codes[at]
            scales[p, pl.ds(k, 1), :] = code_scales[pl.ds(at, 1), :]
        for src, dst, ss, rs in (
            (scales, arrived_scales, send2, recv2),
            (out, arrived, send3, recv3),
        ):
            c = pltpu.make_async_remote_copy(
                src_ref=src.at[p],
                dst_ref=dst.at[me],
                send_sem=ss.at[q],
                recv_sem=rs.at[q],
                device_id={"dev": p},
                device_id_type=MESH,
            )
            c.start()
            copies.append(c)
    for k in range(CAP):
        at = index_s[PLACE, CAP * (GROUP - 1) + k]
        arrived[me, k] = codes[at]
        arrived_scales[me, pl.ds(k, 1), :] = code_scales[pl.ds(at, 1), :]
    for c in copies:
        c.wait()


def split(value):
    high = value.astype(bf16)
    return high, (value - high.astype(f32)).astype(bf16)


def gather_kernel(incoming, arrived, scales, pair, gram, normal, both):
    normal[...] = jnp.zeros_like(normal)
    both[...] = jnp.zeros_like(both)

    def add(s, c):
        row = incoming[s]

        @pl.when(row >= 0)
        def _():
            scale = scales[lax.div(s, CAP), pl.ds(lax.rem(s, CAP), 1), :]
            code = arrived[s].astype(jnp.int32).astype(f32)
            normal[row] = normal[row] + code * scale

        return c

    lax.fori_loop(0, SLOTS, add, 0)
    per = normal.shape[0] // CHUNKS

    def accumulate(g, c):
        high, low = split(normal[pl.ds(g * per, per)].reshape(per * BLK, BLK))
        value = jnp.concatenate([high, low], axis=1)
        pair[pl.ds(pl.multiple_of(g * (per * BLK), per * BLK), per * BLK), :] = value
        both[...] += lax.dot_general(
            high, value, (((0,), (0,)), ((), ())), preferred_element_type=f32
        )
        return c

    lax.fori_loop(0, CHUNKS, accumulate, 0)
    cross = both[:, BLK:]
    gram[...] = (both[:, :BLK] + cross + cross.T).reshape(gram.shape)


def reduce_kernel(voxels, mine, total, first, part, second, s1, r1, s2, r2, s3, r3):
    me = lax.axis_index("dev")
    grp = lax.axis_index("grp")
    groups = lax.axis_size("grp")
    barrier = pltpu.get_barrier_semaphore()
    for dx, dz in OFFSETS:
        pl.semaphore_signal(
            barrier, inc=1, device_id={"dev": peer_of(me, dx, dz)}, device_id_type=MESH
        )
    for o in range(1, groups):
        pl.semaphore_signal(
            barrier, inc=1, device_id={"grp": lax.rem(grp + o, groups)}, device_id_type=MESH
        )
    pl.semaphore_wait(barrier, GROUP - 1 + groups - 1)

    copies = []
    for i, (dx, dz) in enumerate(OFFSETS):
        p = peer_of(me, dx, dz)
        c = pltpu.make_async_remote_copy(
            src_ref=mine.at[p],
            dst_ref=first.at[me],
            send_sem=s1.at[i],
            recv_sem=r1.at[i],
            device_id={"dev": p},
            device_id_type=MESH,
        )
        c.start()
        copies.append(c)
    first[me] = mine[me]
    for c in copies:
        c.wait()
    chunk = first[0]
    for p in range(1, GROUP):
        chunk = chunk + first[p]
    part[...] = chunk

    copies = []
    for o in range(1, groups):
        g = lax.rem(grp + o, groups)
        c = pltpu.make_async_remote_copy(
            src_ref=part,
            dst_ref=second.at[grp],
            send_sem=s2.at[o - 1],
            recv_sem=r2.at[o - 1],
            device_id={"grp": g},
            device_id_type=MESH,
        )
        c.start()
        copies.append(c)
    second[grp] = chunk
    for c in copies:
        c.wait()
    chunk = second[0]
    for g in range(1, groups):
        chunk = chunk + second[g]
    total[me] = chunk / voxels

    copies = []
    for i, (dx, dz) in enumerate(OFFSETS):
        p = peer_of(me, dx, dz)
        c = pltpu.make_async_remote_copy(
            src_ref=total.at[me],
            dst_ref=total.at[me],
            send_sem=s3.at[i],
            recv_sem=r3.at[i],
            device_id={"dev": p},
            device_id_type=MESH,
        )
        c.start()
        copies.append(c)
    for c in copies:
        c.wait()


def factor(gram):
    n = gram.shape[0]
    bands = n // 8
    shape = (8, n)
    row_id = lax.broadcasted_iota(jnp.int32, shape, 0)
    lane_id = lax.broadcasted_iota(jnp.int32, shape, 1)
    g = [gram[8 * b : 8 * b + 8, :] for b in range(bands)]
    w = [jnp.where(lane_id == row_id + 8 * b, 1.0, 0.0).astype(f32) for b in range(bands)]
    r_bands, w_bands = [], []
    for b in range(bands):
        cols = [
            [jnp.broadcast_to(g[t][:, 8 * b + k : 8 * b + k + 1], shape) for k in range(8)]
            for t in range(b, bands)
        ]
        cols[0] = [jnp.where(lane_id < n, c, 0.0) for c in cols[0]]
        pivots = jnp.ones(shape, f32)
        for k in range(8):
            pivot = jnp.broadcast_to(cols[0][k][k : k + 1, :], shape)
            scale = 1.0 / pivot
            pivots = jnp.where(row_id == k, pivot, pivots)
            g_s = jnp.broadcast_to(g[b][k : k + 1, :], shape) * scale
            w_s = jnp.broadcast_to(w[b][k : k + 1, :], shape) * scale
            c_s = {
                j: jnp.broadcast_to(cols[0][j][k : k + 1, :], shape) * scale
                for j in range(k + 1, 8)
            }
            for t in range(b, bands):
                own = cols[t - b]
                f = own[k]
                if t == b:
                    if k == 7:
                        continue
                    f = jnp.where(row_id > k, f, 0.0)
                for j in range(k + 1, 8):
                    own[j] = own[j] - f * c_s[j]
                g[t] = g[t] - f * g_s
                w[t] = w[t] - f * w_s
        root = 1.0 / jnp.sqrt(pivots)
        r_bands.append(jnp.where(lane_id >= row_id + 8 * b, g[b] * root, 0.0))
        w_bands.append(w[b] * root)
    return jnp.concatenate(r_bands, axis=0), jnp.concatenate(w_bands, axis=0)


def basis_kernel(total, pair, basis, r_factor, inverse, made, sem):
    rows = lax.broadcasted_iota(jnp.int32, (BLK, BLK), 0)
    cols = lax.broadcasted_iota(jnp.int32, (BLK, BLK), 1)
    gram = total[...].reshape(BLK, BLK)
    gram = gram + jnp.where(rows == cols, gram_shift, 0.0).astype(f32)
    r_value, lower_inverse = factor(gram)
    r_factor[...] = r_value
    high, low = split(lower_inverse.T)
    inverse[:BLK, :BLK] = high
    inverse[BLK:, :BLK] = high
    inverse[:BLK, BLK:] = low
    inverse[BLK:, BLK:] = jnp.zeros_like(low)
    step = made.shape[0] // CHUNKS

    def chunk(i):
        part = pl.ds(pl.multiple_of(i * step, step), step)
        return part, pltpu.make_async_copy(made.at[part], basis.at[part], sem.at[i])

    def multiply(i, c):
        part, copy = chunk(i)
        value = jnp.dot(pair[part, :], inverse[...], preferred_element_type=f32)
        made[part, :] = value[:, :BLK] + value[:, BLK:]
        copy.start()
        return c

    def finish(i, c):
        chunk(i)[1].wait()
        return c

    lax.fori_loop(0, CHUNKS, multiply, 0)
    lax.fori_loop(0, CHUNKS, finish, 0)


def local(tiles, tile_ray, tile_col, touched, home, sketch):
    block_count = sketch.shape[0] // BLK
    ntouch = touched.shape[0]
    ntiles = tiles.shape[0]
    groups = lax.axis_size("grp")
    i32 = jnp.int32
    dma = pltpu.SemaphoreType.DMA
    peers = GROUP - 1

    arrived, arrived_scales, incoming = pl.pallas_call(
        functools.partial(cycle_kernel, block_count),
        out_shape=(
            jax.ShapeDtypeStruct((GROUP, CAP, BLK, BLK), jnp.int16),
            jax.ShapeDtypeStruct((GROUP, 8, BLK), f32),
            jax.ShapeDtypeStruct((SLOTS,), i32),
        ),
        in_specs=[sm(), sm(), sm(), sm(), hbm(), hbm()],
        out_specs=(vm(), vm(), sm()),
        scratch_shapes=[
            VMEM((block_count, BLK, BLK), bf16),
            VMEM((ntiles + 1, BLK, BLK), bf16),
            VMEM((8, BLK), i32),
            VMEM((GROUP, 8, BLK), i32),
            SMEM((GROUP, 8, BLK), i32),
            VMEM((RB_DEV + 8, BLK), i32),
            SMEM((RB_DEV + 8, BLK), i32),
            SMEM((GROUP,), i32),
            SMEM((GROUP,), i32),
            VMEM((GROUP, CAP, BLK, BLK), bf16),
            VMEM((CAP * STAGES[0], BLK, BLK), bf16),
            VMEM((CAP * (STAGES[1] - STAGES[0]), BLK, BLK), bf16),
            VMEM((CAP * (STAGES[2] - STAGES[1]), BLK, BLK), bf16),
            VMEM((ntouch * BLK, BLK), bf16),
            VMEM((RB_DEV * BLK, BLK), f32),
            VMEM((BLK, RB_DEV * BLK), bf16),
            VMEM((ntouch, BLK, BLK), jnp.int16),
            VMEM((ntouch, BLK), f32),
            VMEM((GROUP, CAP, BLK, BLK), jnp.int16),
            VMEM((GROUP, 8, BLK), f32),
        ]
        + [dma((peers,))] * 8
        + [dma((CHUNKS,)), dma, dma, dma],
        compiler_params=pltpu.CompilerParams(collective_id=1, has_side_effects=True),
        name="cycle",
    )(touched, home, tile_ray, tile_col, sketch.reshape(block_count, BLK, BLK), tiles)

    rows = block_count * BLK
    came = (incoming, arrived.reshape(SLOTS, BLK, BLK), arrived_scales)
    pair, gram = pl.pallas_call(
        gather_kernel,
        out_shape=(
            jax.ShapeDtypeStruct((rows, 2 * BLK), bf16),
            jax.ShapeDtypeStruct((GROUP, BLK // GROUP, BLK), f32),
        ),
        in_specs=[sm(), vm(), vm()],
        out_specs=(vm(), vm()),
        scratch_shapes=[VMEM((block_count, BLK, BLK), f32), VMEM((BLK, 2 * BLK), f32)],
        compiler_params=pltpu.CompilerParams(vmem_limit_bytes=24 << 20),
        name="gather",
    )(*(pltpu.with_memory_space_constraint(v, pltpu.HBM) for v in came))

    voxels = float(sketch.shape[0] * groups * GROUP)
    total = pl.pallas_call(
        functools.partial(reduce_kernel, voxels),
        out_shape=jax.ShapeDtypeStruct((GROUP, BLK // GROUP, BLK), f32),
        in_specs=[vm()],
        out_specs=vm(),
        scratch_shapes=[
            VMEM((GROUP, BLK // GROUP, BLK), f32),
            VMEM((BLK // GROUP, BLK), f32),
            VMEM((groups, BLK // GROUP, BLK), f32),
            dma((peers,)),
            dma((peers,)),
            dma((groups - 1,)),
            dma((groups - 1,)),
            dma((peers,)),
            dma((peers,)),
        ],
        compiler_params=pltpu.CompilerParams(
            collective_id=3, has_side_effects=True, vmem_limit_bytes=8 << 20
        ),
        name="reduce",
    )(gram)

    basis, r_factor = pl.pallas_call(
        basis_kernel,
        out_shape=(
            jax.ShapeDtypeStruct((rows, BLK), f32),
            jax.ShapeDtypeStruct((BLK, BLK), f32),
        ),
        in_specs=[vm(), vm()],
        out_specs=(hbm(), vm()),
        scratch_shapes=[
            VMEM((2 * BLK, 2 * BLK), bf16),
            VMEM((rows, BLK), f32),
            dma((CHUNKS,)),
        ],
        compiler_params=pltpu.CompilerParams(vmem_limit_bytes=24 << 20),
        name="basis",
    )(total, pair)
    return (basis, r_factor)


def solution(mesh):
    in_specs = (
        P(("grp", "dev"), None, None),
        P(("grp", "dev")),
        P(("grp", "dev")),
        P(("grp", "dev")),
        P(),
        P(("grp", "dev"), None),
    )
    out_specs = (P(("grp", "dev"), None), P())
    return jax.shard_map(local, mesh=mesh, in_specs=in_specs, out_specs=out_specs, check_vma=False)
```

```python
import functools

import jax
import jax.numpy as jnp
from jax import lax
from jax.experimental import pallas as pl
from jax.experimental.pallas import tpu as pltpu
from jax.sharding import PartitionSpec as P

CAP = 3
RB_DEV = 32
BLK = 128
SIDE = 4
GROUP = SIDE * SIDE
CHUNKS = 8
PER = 8
STAGES = (12, 14, 16)
ORDER = RB_DEV
PLACE = RB_DEV + 1
COMING = RB_DEV + 2
SLOT = RB_DEV + 3
SLOTS = GROUP * CAP
gram_shift = 0.001
LEVELS = 32767.0
TINY = 1e-30

MESH = pl.DeviceIdType.MESH
SMEM = pltpu.SMEM
VMEM = pltpu.VMEM
f32 = jnp.float32
bf16 = jnp.bfloat16


def vm():
    return pl.BlockSpec(memory_space=VMEM)


def sm():
    return pl.BlockSpec(memory_space=SMEM)


def hbm():
    return pl.BlockSpec(memory_space=pl.ANY)


OFFSETS = sorted(
    [(dx, dz) for dx in range(SIDE) for dz in range(SIDE) if (dx, dz) != (0, 0)],
    key=lambda o: ((min(o[0], SIDE - o[0]) + min(o[1], SIDE - o[1])), o),
)


LEAVING = sorted(
    [(dx, dz) for dx in range(SIDE) for dz in range(SIDE) if (dx, dz) != (0, 0)],
    key=lambda o: (-(min(o[0], SIDE - o[0]) + min(o[1], SIDE - o[1])), o),
)


def peer_of(me, dx, dz):
    x, z = lax.div(me, SIDE), lax.rem(me, SIDE)
    return lax.rem(x + dx, SIDE) * SIDE + lax.rem(z + dz, SIDE)


def cycle_kernel(
    block_count,
    touched_in,
    home_in,
    ray_in,
    col_in,
    sketch_in,
    tiles_in,
    arrived,
    arrived_scales,
    incoming,
    sketch,
    held,
    ask,
    asked,
    asked_s,
    index,
    index_s,
    place_s,
    coming_s,
    packed,
    got_0,
    got_1,
    got_2,
    xc,
    sums,
    images_t,
    codes,
    code_scales,
    out,
    scales,
    asend,
    arecv,
    send,
    recv,
    send2,
    recv2,
    send3,
    recv3,
    tsem,
    ssem,
    lsem,
    isem,
    touched,
    home,
    ray,
    col,
    nsem,
    osem,
):
    me = lax.axis_index("dev")
    ntouch = touched.shape[0]
    ntiles = ray.shape[0]
    i32 = jnp.int32
    numbers = []
    for i, (src, dst) in enumerate(
        ((touched_in, touched), (home_in, home), (ray_in, ray), (col_in, col))
    ):
        c = pltpu.make_async_copy(src, dst, nsem.at[i])
        c.start()
        numbers.append(c)
    whole = pltpu.make_async_copy(sketch_in, sketch, ssem)
    whole.start()
    step = ntiles // CHUNKS
    loads = []
    for i in range(CHUNKS):
        c = pltpu.make_async_copy(
            tiles_in.at[pl.ds(i * step, step)], held.at[pl.ds(i * step, step)], tsem.at[i]
        )
        c.start()
        loads.append(c)
    barrier = pltpu.get_barrier_semaphore()
    for dx, dz in OFFSETS:
        pl.semaphore_signal(
            barrier, inc=1, device_id={"dev": peer_of(me, dx, dz)}, device_id_type=MESH
        )

    for q, (dx, dz) in enumerate(LEAVING + [(0, 0)]):
        place_s[dx * SIDE + dz] = q
    for q, (dx, dz) in enumerate(OFFSETS + [(0, 0)]):
        back = (SIDE - dx) % SIDE * SIDE + (SIDE - dz) % SIDE
        coming_s[back] = (q + 1) % GROUP
    x, z = lax.div(me, SIDE), lax.rem(me, SIDE)
    lane = lax.broadcasted_iota(i32, (8, BLK), 1)
    row = lax.broadcasted_iota(i32, (8, BLK), 0)
    wanted = jnp.full((8, BLK), -1, i32)
    holders, keys, arrivals = [], [], []
    for c in numbers:
        c.wait()
    for j in range(ntouch):
        stored = home[touched[j]]
        holder = lax.rem(lax.div(stored, block_count), GROUP)
        n = i32(0)
        for earlier in holders:
            n = n + (earlier == holder).astype(i32)
        n = jnp.minimum(n, CAP - 1)
        holders.append(holder)
        s = holder * CAP + n
        hx, hz = lax.div(holder, SIDE), lax.rem(holder, SIDE)
        far = lax.rem(hx - x + SIDE, SIDE) * SIDE + lax.rem(hz - z + SIDE, SIDE)
        keys.append(place_s[far] * CAP + n)
        arrivals.append(coming_s[far] * CAP + n)
        wanted = jnp.where(lane == s, lax.rem(stored, block_count), wanted)
    ask[...] = wanted[:1]
    asked[me] = wanted[:1]

    pl.semaphore_wait(barrier, GROUP - 1)
    asks = []
    for i, (dx, dz) in enumerate(LEAVING):
        c = pltpu.make_async_remote_copy(
            src_ref=ask,
            dst_ref=asked.at[me],
            send_sem=asend.at[i],
            recv_sem=arecv.at[i],
            device_id={"dev": peer_of(me, dx, dz)},
            device_id_type=MESH,
        )
        c.start()
        asks.append(c)

    order = jnp.zeros((8, BLK), i32)
    for j in range(ntouch):
        rank = i32(0)
        for k in range(ntouch):
            if k != j:
                rank = rank + (keys[k] < keys[j]).astype(i32)
        order = jnp.where((row == 0) & (lane == rank), j, order)
        order = jnp.where((row == 1) & (lane == keys[j]), rank, order)
        rank = i32(0)
        for k in range(ntouch):
            if k != j:
                rank = rank + (arrivals[k] < arrivals[j]).astype(i32)
        order = jnp.where((row == 2) & (lane == rank), j, order)
        order = jnp.where((row == 3) & (lane == j), arrivals[j], order)
    index[pl.ds(RB_DEV, 8), :] = order

    bands = RB_DEV // 8
    pairs = [
        jnp.where(lane < ntouch, (row + 8 * b) * ntouch + lane, -1) for b in range(bands)
    ]

    def place(t, table):
        pair = ray[t] * ntouch + col[t]
        return tuple(jnp.where(p == pair, t, v) for p, v in zip(pairs, table))

    table = lax.fori_loop(
        0, ntiles, place, (jnp.full((8, BLK), ntiles, i32),) * bands, unroll=8
    )
    for b in range(bands):
        index[pl.ds(8 * b, 8), :] = table[b]
    tables = pltpu.make_async_copy(index, index_s, isem)
    tables.start()
    held[ntiles] = jnp.zeros((BLK, BLK), bf16)

    whole.wait()
    for c in asks:
        c.wait()
    local = pltpu.make_async_copy(asked, asked_s, lsem)
    local.start()
    local.wait()

    got = (got_0, got_1, got_2)
    copies = []
    for i, (dx, dz) in enumerate(OFFSETS):
        p = peer_of(me, dx, dz)
        stage = sum(i + 1 >= owners for owners in STAGES)
        first = (0, *STAGES)[stage]
        for k in range(CAP):
            packed[p, k] = sketch[jnp.maximum(asked_s[p, 0, CAP * me + k], 0)]
        c = pltpu.make_async_remote_copy(
            src_ref=packed.at[p],
            dst_ref=got[stage].at[pl.ds(CAP * (i + 1 - first), CAP)],
            send_sem=send.at[i],
            recv_sem=recv.at[i],
            device_id={"dev": p},
            device_id_type=MESH,
        )
        c.start()
        copies.append(c)
    for k in range(CAP):
        got_0[k] = sketch[jnp.maximum(asked_s[me, 0, CAP * me + k], 0)]
    for p in range(GROUP):
        for k in range(CAP):
            incoming[CAP * p + k] = asked_s[p, 0, CAP * me + k]
    tables.wait()
    for c in loads:
        c.wait()

    received = 0
    begin = 0
    for owners in STAGES:
        for c in copies[received : owners - 1]:
            c.wait_recv()
        received = owners - 1
        end = max(begin, CAP * owners - (SLOTS - ntouch))
        cols = [index_s[COMING, i] for i in range(begin, end)]
        for i, c in enumerate(cols):
            at = index_s[SLOT, c]
            block = got_0[jnp.minimum(at, CAP * STAGES[0] - 1)]
            for stage in range(1, len(STAGES)):
                if STAGES[stage] <= owners:
                    low, high = CAP * STAGES[stage - 1], CAP * STAGES[stage]
                    later = got[stage][jnp.clip(at - low, 0, high - low - 1)]
                    block = jnp.where(at >= low, later, block)
            xc[pl.ds((begin + i) * BLK, BLK), :] = block

        def image_step(g, carry, cols=cols, begin=begin, end=end, last=owners == GROUP):
            rows = [
                jnp.concatenate([held[index_s[g * PER + i, c]] for c in cols], axis=1)
                for i in range(PER)
            ]
            lhs = jnp.concatenate(rows, axis=0)
            known = xc[pl.ds(begin * BLK, (end - begin) * BLK), :]
            image = jnp.dot(lhs, known, preferred_element_type=f32)
            start = pl.multiple_of(g * (PER * BLK), PER * BLK)
            if begin > 0:
                image = image + sums[pl.ds(start, PER * BLK), :]
            if last:
                images_t[:, pl.ds(start, PER * BLK)] = image.T.astype(bf16)
            else:
                sums[pl.ds(start, PER * BLK), :] = image
            return carry

        lax.fori_loop(0, RB_DEV // PER, image_step, 0)
        begin = end
    for c in copies:
        c.wait_send()

    def normal_step(g, carry):
        cols = []
        for i in range(2):
            c = index_s[ORDER, 2 * g + i]
            cols.append(
                jnp.concatenate([held[index_s[r, c]] for r in range(RB_DEV)], axis=0)
            )
        rhs = jnp.concatenate(cols, axis=1)
        part = jnp.dot(images_t[...], rhs, preferred_element_type=f32)
        for i in range(2):
            block = part[:, i * BLK : (i + 1) * BLK].T
            top = jnp.maximum(jnp.max(jnp.abs(block), axis=0, keepdims=True), TINY)
            code = jnp.round(block * (LEVELS / top))
            codes[2 * g + i] = code.astype(i32).astype(jnp.int16)
            code_scales[pl.ds(2 * g + i, 1), :] = top * (1.0 / LEVELS)
        return carry

    copies = []
    done = 0
    for q in range(GROUP - 1):
        until = -(-min(ntouch, CAP * (q + 1)) // 2)
        if until > done:
            lax.fori_loop(done, until, normal_step, 0)
            done = until
        p = peer_of(me, *LEAVING[q])
        for k in range(CAP):
            at = index_s[PLACE, CAP * q + k]
            out[p, k] = codes[at]
            scales[p, pl.ds(k, 1), :] = code_scales[pl.ds(at, 1), :]
        for src, dst, ss, rs in (
            (scales, arrived_scales, send2, recv2),
            (out, arrived, send3, recv3),
        ):
            c = pltpu.make_async_remote_copy(
                src_ref=src.at[p],
                dst_ref=dst.at[me],
                send_sem=ss.at[q],
                recv_sem=rs.at[q],
                device_id={"dev": p},
                device_id_type=MESH,
            )
            c.start()
            copies.append(c)
    for k in range(CAP):
        at = index_s[PLACE, CAP * (GROUP - 1) + k]
        out[me, k] = codes[at]
        arrived_scales[me, pl.ds(k, 1), :] = code_scales[pl.ds(at, 1), :]
    own = pltpu.make_async_copy(out.at[me], arrived.at[me], osem)
    own.start()
    copies.append(own)
    for c in copies:
        c.wait()


def split(value):
    high = value.astype(bf16)
    return high, (value - high.astype(f32)).astype(bf16)


def gather_kernel(incoming, arrived_in, scales, pair, gram, normal, both, arrived, sem):
    fetch = pltpu.make_async_copy(arrived_in, arrived, sem)
    fetch.start()
    normal[...] = jnp.zeros_like(normal)
    both[...] = jnp.zeros_like(both)

    def add(s, c):
        row = incoming[s]

        @pl.when(row >= 0)
        def _():
            scale = scales[lax.div(s, CAP), pl.ds(lax.rem(s, CAP), 1), :]
            code = arrived[s].astype(jnp.int32).astype(f32)
            normal[row] = normal[row] + code * scale

        return c

    fetch.wait()
    lax.fori_loop(0, SLOTS, add, 0)
    per = normal.shape[0] // CHUNKS

    def accumulate(g, c):
        high, low = split(normal[pl.ds(g * per, per)].reshape(per * BLK, BLK))
        value = jnp.concatenate([high, low], axis=1)
        pair[pl.ds(pl.multiple_of(g * (per * BLK), per * BLK), per * BLK), :] = value
        both[...] += lax.dot_general(
            high, value, (((0,), (0,)), ((), ())), preferred_element_type=f32
        )
        return c

    lax.fori_loop(0, CHUNKS, accumulate, 0)
    cross = both[:, BLK:]
    gram[...] = (both[:, :BLK] + cross + cross.T).reshape(gram.shape)


def reduce_kernel(voxels, mine, total, first, part, second, s1, r1, s2, r2, s3, r3):
    me = lax.axis_index("dev")
    grp = lax.axis_index("grp")
    groups = lax.axis_size("grp")
    barrier = pltpu.get_barrier_semaphore()
    for dx, dz in OFFSETS:
        pl.semaphore_signal(
            barrier, inc=1, device_id={"dev": peer_of(me, dx, dz)}, device_id_type=MESH
        )
    for o in range(1, groups):
        pl.semaphore_signal(
            barrier, inc=1, device_id={"grp": lax.rem(grp + o, groups)}, device_id_type=MESH
        )
    pl.semaphore_wait(barrier, GROUP - 1 + groups - 1)

    copies = []
    for i, (dx, dz) in enumerate(LEAVING):
        p = peer_of(me, dx, dz)
        c = pltpu.make_async_remote_copy(
            src_ref=mine.at[p],
            dst_ref=first.at[me],
            send_sem=s1.at[i],
            recv_sem=r1.at[i],
            device_id={"dev": p},
            device_id_type=MESH,
        )
        c.start()
        copies.append(c)
    first[me] = mine[me]
    for c in copies:
        c.wait()
    chunk = first[0]
    for p in range(1, GROUP):
        chunk = chunk + first[p]
    part[...] = chunk

    copies = []
    for o in range(1, groups):
        g = lax.rem(grp + o, groups)
        c = pltpu.make_async_remote_copy(
            src_ref=part,
            dst_ref=second.at[grp],
            send_sem=s2.at[o - 1],
            recv_sem=r2.at[o - 1],
            device_id={"grp": g},
            device_id_type=MESH,
        )
        c.start()
        copies.append(c)
    second[grp] = chunk
    for c in copies:
        c.wait()
    chunk = second[0]
    for g in range(1, groups):
        chunk = chunk + second[g]
    total[me] = chunk / voxels

    copies = []
    for i, (dx, dz) in enumerate(LEAVING):
        p = peer_of(me, dx, dz)
        c = pltpu.make_async_remote_copy(
            src_ref=total.at[me],
            dst_ref=total.at[me],
            send_sem=s3.at[i],
            recv_sem=r3.at[i],
            device_id={"dev": p},
            device_id_type=MESH,
        )
        c.start()
        copies.append(c)
    for c in copies:
        c.wait()


def factor(gram):
    n = gram.shape[0]
    bands = n // 8
    shape = (8, n)
    row_id = lax.broadcasted_iota(jnp.int32, shape, 0)
    lane_id = lax.broadcasted_iota(jnp.int32, shape, 1)
    g = [gram[8 * b : 8 * b + 8, :] for b in range(bands)]
    w = [jnp.where(lane_id == row_id + 8 * b, 1.0, 0.0).astype(f32) for b in range(bands)]
    r_bands, w_bands = [], []
    for b in range(bands):
        cols = [
            [jnp.broadcast_to(g[t][:, 8 * b + k : 8 * b + k + 1], shape) for k in range(8)]
            for t in range(b, bands)
        ]
        cols[0] = [jnp.where(lane_id < n, c, 0.0) for c in cols[0]]
        pivots = jnp.ones(shape, f32)
        for k in range(8):
            pivot = jnp.broadcast_to(cols[0][k][k : k + 1, :], shape)
            scale = 1.0 / pivot
            pivots = jnp.where(row_id == k, pivot, pivots)
            g_s = jnp.broadcast_to(g[b][k : k + 1, :], shape) * scale
            w_s = jnp.broadcast_to(w[b][k : k + 1, :], shape) * scale
            c_s = {
                j: jnp.broadcast_to(cols[0][j][k : k + 1, :], shape) * scale
                for j in range(k + 1, 8)
            }
            for t in range(b, bands):
                own = cols[t - b]
                f = own[k]
                if t == b:
                    if k == 7:
                        continue
                    f = jnp.where(row_id > k, f, 0.0)
                for j in range(k + 1, 8):
                    own[j] = own[j] - f * c_s[j]
                g[t] = g[t] - f * g_s
                w[t] = w[t] - f * w_s
        root = 1.0 / jnp.sqrt(pivots)
        r_bands.append(jnp.where(lane_id >= row_id + 8 * b, g[b] * root, 0.0))
        w_bands.append(w[b] * root)
    return jnp.concatenate(r_bands, axis=0), jnp.concatenate(w_bands, axis=0)


def basis_kernel(total, pair, basis, r_factor, inverse, made, sem):
    rows = lax.broadcasted_iota(jnp.int32, (BLK, BLK), 0)
    cols = lax.broadcasted_iota(jnp.int32, (BLK, BLK), 1)
    gram = total[...].reshape(BLK, BLK)
    gram = gram + jnp.where(rows == cols, gram_shift, 0.0).astype(f32)
    r_value, lower_inverse = factor(gram)
    r_factor[...] = r_value
    high, low = split(lower_inverse.T)
    inverse[:BLK, :BLK] = high
    inverse[BLK:, :BLK] = high
    inverse[:BLK, BLK:] = low
    inverse[BLK:, BLK:] = jnp.zeros_like(low)
    step = made.shape[0] // CHUNKS

    def chunk(i):
        part = pl.ds(pl.multiple_of(i * step, step), step)
        return part, pltpu.make_async_copy(made.at[part], basis.at[part], sem.at[i])

    def multiply(i, c):
        part, copy = chunk(i)
        value = jnp.dot(pair[part, :], inverse[...], preferred_element_type=f32)
        made[part, :] = value[:, :BLK] + value[:, BLK:]
        copy.start()
        return c

    def finish(i, c):
        chunk(i)[1].wait()
        return c

    lax.fori_loop(0, CHUNKS, multiply, 0)
    lax.fori_loop(0, CHUNKS, finish, 0)


def local(tiles, tile_ray, tile_col, touched, home, sketch):
    block_count = sketch.shape[0] // BLK
    ntouch = touched.shape[0]
    ntiles = tiles.shape[0]
    groups = lax.axis_size("grp")
    i32 = jnp.int32
    dma = pltpu.SemaphoreType.DMA
    peers = GROUP - 1

    arrived, arrived_scales, incoming = pl.pallas_call(
        functools.partial(cycle_kernel, block_count),
        out_shape=(
            jax.ShapeDtypeStruct((GROUP, CAP, BLK, BLK), jnp.int16),
            jax.ShapeDtypeStruct((GROUP, 8, BLK), f32),
            jax.ShapeDtypeStruct((SLOTS,), i32),
        ),
        in_specs=[hbm()] * 6,
        out_specs=(pl.BlockSpec(memory_space=pltpu.HBM), vm(), sm()),
        scratch_shapes=[
            VMEM((block_count, BLK, BLK), bf16),
            VMEM((ntiles + 1, BLK, BLK), bf16),
            VMEM((1, BLK), i32),
            VMEM((GROUP, 1, BLK), i32),
            SMEM((GROUP, 1, BLK), i32),
            VMEM((RB_DEV + 8, BLK), i32),
            SMEM((RB_DEV + 8, BLK), i32),
            SMEM((GROUP,), i32),
            SMEM((GROUP,), i32),
            VMEM((GROUP, CAP, BLK, BLK), bf16),
            VMEM((CAP * STAGES[0], BLK, BLK), bf16),
            VMEM((CAP * (STAGES[1] - STAGES[0]), BLK, BLK), bf16),
            VMEM((CAP * (STAGES[2] - STAGES[1]), BLK, BLK), bf16),
            VMEM((ntouch * BLK, BLK), bf16),
            VMEM((RB_DEV * BLK, BLK), f32),
            VMEM((BLK, RB_DEV * BLK), bf16),
            VMEM((ntouch, BLK, BLK), jnp.int16),
            VMEM((ntouch, BLK), f32),
            VMEM((GROUP, CAP, BLK, BLK), jnp.int16),
            VMEM((GROUP, 8, BLK), f32),
        ]
        + [dma((peers,))] * 8
        + [dma((CHUNKS,)), dma, dma, dma]
        + [SMEM(v.shape, i32) for v in (touched, home, tile_ray, tile_col)]
        + [dma((4,)), dma],
        compiler_params=pltpu.CompilerParams(collective_id=1, has_side_effects=True),
        name="cycle",
    )(touched, home, tile_ray, tile_col, sketch.reshape(block_count, BLK, BLK), tiles)

    rows = block_count * BLK
    came = (incoming, arrived.reshape(SLOTS, BLK, BLK), arrived_scales)
    pair, gram = pl.pallas_call(
        gather_kernel,
        out_shape=(
            jax.ShapeDtypeStruct((rows, 2 * BLK), bf16),
            jax.ShapeDtypeStruct((GROUP, BLK // GROUP, BLK), f32),
        ),
        in_specs=[sm(), hbm(), vm()],
        out_specs=(vm(), vm()),
        scratch_shapes=[
            VMEM((block_count, BLK, BLK), f32),
            VMEM((BLK, 2 * BLK), f32),
            VMEM((SLOTS, BLK, BLK), jnp.int16),
            dma,
        ],
        compiler_params=pltpu.CompilerParams(vmem_limit_bytes=24 << 20),
        name="gather",
    )(*(pltpu.with_memory_space_constraint(v, pltpu.HBM) for v in came))

    voxels = float(sketch.shape[0] * groups * GROUP)
    total = pl.pallas_call(
        functools.partial(reduce_kernel, voxels),
        out_shape=jax.ShapeDtypeStruct((GROUP, BLK // GROUP, BLK), f32),
        in_specs=[vm()],
        out_specs=vm(),
        scratch_shapes=[
            VMEM((GROUP, BLK // GROUP, BLK), f32),
            VMEM((BLK // GROUP, BLK), f32),
            VMEM((groups, BLK // GROUP, BLK), f32),
            dma((peers,)),
            dma((peers,)),
            dma((groups - 1,)),
            dma((groups - 1,)),
            dma((peers,)),
            dma((peers,)),
        ],
        compiler_params=pltpu.CompilerParams(
            collective_id=3, has_side_effects=True, vmem_limit_bytes=8 << 20
        ),
        name="reduce",
    )(gram)

    basis, r_factor = pl.pallas_call(
        basis_kernel,
        out_shape=(
            jax.ShapeDtypeStruct((rows, BLK), f32),
            jax.ShapeDtypeStruct((BLK, BLK), f32),
        ),
        in_specs=[vm(), vm()],
        out_specs=(hbm(), vm()),
        scratch_shapes=[
            VMEM((2 * BLK, 2 * BLK), bf16),
            VMEM((rows, BLK), f32),
            dma((CHUNKS,)),
        ],
        compiler_params=pltpu.CompilerParams(vmem_limit_bytes=24 << 20),
        name="basis",
    )(total, pair)
    return (basis, r_factor)


def solution(mesh):
    in_specs = (
        P(("grp", "dev"), None, None),
        P(("grp", "dev")),
        P(("grp", "dev")),
        P(("grp", "dev")),
        P(),
        P(("grp", "dev"), None),
    )
    out_specs = (P(("grp", "dev"), None), P())
    return jax.shard_map(local, mesh=mesh, in_specs=in_specs, out_specs=out_specs, check_vma=False)
```
